32 devices in a mesh: gx: 8 (over z, x), gy: 4 (over y, core).
Axes of the slice: x: 2, y: 2, z: 4, core: 2. Of those that a mesh axis runs over, the one named last changes fastest.
Arguments:
- forcing: float32 [3, 64, 64, 512], P(None, 'gx', 'gy'), may hold values from -6.5 to 6.5
- phase_ids: int32 [64, 64, 512], P('gx', 'gy'), may hold values from 0 to 3
Outputs:
- velocity: float32 [3, 64, 64, 512], P(None, 'gx', 'gy')
The draws below stay inside these ranges and needn't reach their ends.
All inputs are finite; a program needn't handle non-finite values.
Results may differ from the reference program's by a relative error of at most 0.0003.
Values sent between devices are 32-bit elements; how exact they have to be, the bound alone decides.
A program may use at most 128 MiB of HBM per device.

```python
import jax
import jax.numpy as jnp
from jax import lax

NZ = 512
COARSE_SWEEPS = 6
NX = 64
NY = 64


def draw_forcing(key, part):
    base = jax.random.normal(key, (3, NX, NY, NZ), jnp.float32)
    return jnp.clip(base, -6.0, 6.0)


def with_ends(array, key, low, top_value):
    shape = array.shape
    place = [jax.random.randint(jax.random.fold_in(key, axis), (), 0, shape[axis]) for axis in range(len(shape))]
    array = array.at[tuple(place)].set(low)
    longest = shape.index(max(shape))
    place[longest] = (place[longest] + 1) % shape[longest]
    return array.at[tuple(place)].set(top_value)


def setup_inputs(seed: int = 0) -> dict:
    arg_keys = jax.random.split(jax.random.key(seed), 3)
    forcing = draw_forcing(jax.random.fold_in(arg_keys[2], 71), 0)
    phase_ids = with_ends(jax.random.randint(arg_keys[1], (NX, NY, NZ), 0, 4), jax.random.fold_in(arg_keys[1], 1), 0, 3).astype(jnp.int32)
    return {"forcing": forcing, "phase_ids": phase_ids}


viscosities = (0.2, 0.6, 1.5, 4.0)
relax_weight = 2.0 / 3.0


def lookup(phase_ids):
    viscosity = jnp.zeros(phase_ids.shape, jnp.float32)
    for material, visc_value in enumerate(viscosities):
        viscosity = viscosity + jnp.where(phase_ids == material, jnp.float32(visc_value), jnp.float32(0.0))
    return viscosity


def restrict(values):
    extent = values.shape
    leading = extent[:-3]
    blocks = values.reshape(leading + (extent[-3] // 2, 2, extent[-2] // 2, 2, extent[-1] // 2, 2))
    return jnp.mean(blocks, axis=(-5, -3, -1))


def prolong(values):
    return jnp.repeat(jnp.repeat(jnp.repeat(values, 2, axis=-3), 2, axis=-2), 2, axis=-1)


def pad_plane(values, width):
    padding = [(0, 0)] * (values.ndim - 3) + [(width, width), (width, width), (0, 0)]
    return jnp.pad(values, padding)


def face_set(wide_visc, spacing):
    center = wide_visc[1:-1, 1:-1, :]
    z_padded = jnp.pad(center, ((0, 0), (0, 0), (1, 1)))
    besides = (wide_visc[2:, 1:-1, :], wide_visc[:-2, 1:-1, :], wide_visc[1:-1, 2:, :],
               wide_visc[1:-1, :-2, :], z_padded[:, :, 2:], z_padded[:, :, :-2])
    coeffs = tuple(jnp.where(beside > 0.0, 0.5 * (center + beside), center) / spacing for beside in besides)
    diagonal = coeffs[0]
    for entry in coeffs[1:]:
        diagonal = diagonal + entry
    inside = center > 0.0
    inverse = jnp.where(inside, 1.0 / jnp.where(inside, diagonal, 1.0), 0.0)
    return coeffs, inverse


def apply_operator(wide_field, coeffs):
    center = wide_field[..., 1:-1, 1:-1, :]
    padding = [(0, 0)] * (center.ndim - 1) + [(1, 1)]
    z_padded = jnp.pad(center, padding)
    besides = (wide_field[..., 2:, 1:-1, :], wide_field[..., :-2, 1:-1, :], wide_field[..., 1:-1, 2:, :],
               wide_field[..., 1:-1, :-2, :], z_padded[..., 2:], z_padded[..., :-2])
    summed = jnp.zeros_like(center)
    for face_coeff, beside in zip(coeffs, besides):
        summed = summed + face_coeff * (center - beside)
    return summed


def reference(forcing, phase_ids):
    viscosity = lookup(phase_ids)
    level_sets = []
    for level_index in range(3):
        level_sets.append(face_set(pad_plane(viscosity, 1), 4.0 ** level_index))
        if level_index < 2:
            viscosity = restrict(viscosity)

    def jacobi_sweep(current, source, level_set):
        coeffs, inverse = level_set
        return current + relax_weight * (source - apply_operator(pad_plane(current, 1), coeffs)) * inverse

    def descend(source, level_set):
        coeffs, inverse = level_set
        current = relax_weight * source * inverse
        current = jacobi_sweep(current, source, level_set)
        residual = source - apply_operator(pad_plane(current, 1), coeffs)
        return current, restrict(residual)

    def single(source):
        fine_velocity, source_one = descend(source, level_sets[0])
        middle, source_two = descend(source_one, level_sets[1])
        coarse = relax_weight * source_two * level_sets[2][1]
        for repeat in range(COARSE_SWEEPS - 1):
            coarse = jacobi_sweep(coarse, source_two, level_sets[2])
        middle = middle + prolong(coarse)
        middle = jacobi_sweep(middle, source_one, level_sets[1])
        middle = jacobi_sweep(middle, source_one, level_sets[1])
        fine_velocity = fine_velocity + prolong(middle)
        fine_velocity = jacobi_sweep(fine_velocity, source, level_sets[0])
        fine_velocity = jacobi_sweep(fine_velocity, source, level_sets[0])
        return fine_velocity

    return lax.map(single, forcing)
```

```python
import functools

import jax
import jax.numpy as jnp
from jax import lax
from jax.experimental import pallas as pl
from jax.experimental.pallas import tpu as pltpu
from jax.sharding import PartitionSpec as P

COARSE_SWEEPS = 6
VISCOSITIES = (0.2, 0.6, 1.5, 4.0)
WEIGHT = 2.0 / 3.0
MESH = pl.DeviceIdType.MESH
WINDOW = [(dx, dy) for dx in range(-2, 3) for dy in range(-1, 2) if (dx, dy) != (0, 0)]
TOP = 8


def up8(n):
    return -(-n // 8) * 8


def side_slices(step, first, length, lo, hi):
    if step > 0:
        return (first + length - hi, first - hi)
    return (first + lo - 1, first + length + lo - 1)


class Kernel:
    def __init__(self, sizes, comps, grid):
        self.X, self.Y, self.Z = sizes
        self.C = comps
        self.grid = grid
        self.scratch = {}
        self.n_sems = 0
        self.plan()

    def buf(self, name, shape, dtype=jnp.float32):
        self.scratch[name] = pltpu.VMEM(tuple(shape), dtype)

    def halo(self, name, target, comps, px, X, Y, Z, lo, hi, diag):
        w = hi - lo + 1
        msgs = []
        for dx in (1, -1):
            s, d = side_slices(dx, px, X, lo, hi)
            msgs.append(("x", dx, 0, s, d, self.n_sems))
            self.n_sems += 1
        n = comps * X * w
        self.buf(name + "_sy", (2, up8(n), Z))
        self.buf(name + "_ry", (2, up8(n), Z))
        for k, dy in enumerate((1, -1)):
            s, d = side_slices(dy, TOP, Y, lo, hi)
            msgs.append(("y", k, dy, s, d, self.n_sems))
            self.n_sems += 1
        if diag:
            n = comps * diag * diag
            self.buf(name + "_sd", (4, up8(n), Z))
            self.buf(name + "_rd", (4, up8(n), Z))
            for k, (dx, dy) in enumerate([(1, 1), (1, -1), (-1, 1), (-1, -1)]):
                msgs.append(("d", k, (dx, dy), side_slices(dx, px, X, 1, diag),
                             side_slices(dy, TOP, Y, 1, diag), self.n_sems))
                self.n_sems += 1
        return dict(name=name, target=target, comps=comps, px=px, X=X, Y=Y, w=w, diag=diag, msgs=msgs)

    def plan(self):
        X, Y, Z, C = self.X, self.Y, self.Z, self.C
        self.P0, self.R0 = X + 4, Y + 16
        self.X1, self.Y1, self.Z1 = X // 2, Y // 2, Z // 2
        self.P1, self.R1 = self.X1 + 6, self.Y1 + 16
        self.X2, self.Y2, self.Z2 = X // 4, Y // 4, Z // 4
        self.P2, self.R2 = self.X2 + 8, up8(self.Y2 * 3)
        b = self.buf
        b("ph", (X, Y, Z), jnp.int32)
        b("E0", (1, self.P0, self.R0, Z))
        b("C0", (8, self.P0, self.R0, Z))
        for n in ("F0", "A0", "V0", "B0"):
            b(n, (C, self.P0, self.R0, Z))
        b("O0", (C, X, Y, Z))
        b("T0", (C * self.X1 * Y, Z))
        b("E1", (1, self.P1, self.R1, self.Z1))
        b("C1", (8, self.P1, self.R1, self.Z1))
        for n in ("F1", "A1", "V1", "B1"):
            b(n, (C, self.P1, self.R1, self.Z1))
        b("T1", (C * self.X2 * self.Y1, self.Z1))
        b("E2", (1, self.P2, self.R2, self.Z2))
        b("C2", (8, self.P2, self.R2, self.Z2))
        for n in ("F2", "A2", "B2"):
            b(n, (C, self.P2, self.R2, self.Z2))
        blk = self.X2 * self.Y2
        for n, c in (("e2", 1), ("f2", C), ("v2", C)):
            b("S" + n, (c * blk, self.Z2))
            b("R" + n, (len(WINDOW), c * blk, self.Z2))
        b("UZ1", (self.R2 * C * (self.X2 + 4), self.Z1))
        b("UZ0", (self.R1 * C * (self.X1 + 2), self.Z))
        self.hE0 = self.halo("hE0", "E0", 1, 2, X, Y, Z, 1, 2, 1)
        self.hF0 = self.halo("hF0", "F0", C, 2, X, Y, Z, 1, 1, 0)
        self.hV0 = self.halo("hV0", "V0", C, 2, X, Y, Z, 1, 1, 0)
        self.hW0 = self.halo("hW0", "V0", C, 2, X, Y, Z, 2, 2, 1)
        self.hE1 = self.halo("hE1", "E1", 1, 3, self.X1, self.Y1, self.Z1, 1, 3, 3)
        self.hF1 = self.halo("hF1", "F1", C, 3, self.X1, self.Y1, self.Z1, 1, 2, 2)
        self.hV1 = self.halo("hV1", "V1", C, 3, self.X1, self.Y1, self.Z1, 1, 3, 3)
        self.win = {}
        for n in ("e2", "f2", "v2"):
            self.win[n] = self.n_sems
            self.n_sems += len(WINDOW)

    def exists(self, dx, dy):
        ok = None
        for step, me, size in ((dx, self.gx, self.grid[0]), (dy, self.gy, self.grid[1])):
            if step:
                t = (me + step >= 0) & (me + step < size)
                ok = t if ok is None else ok & t
        return ok

    def copy(self, src, dst, sem, dx, dy):
        return pltpu.make_async_remote_copy(
            src_ref=src, dst_ref=dst, send_sem=self.ssem.at[sem], recv_sem=self.rsem.at[sem],
            device_id=(self.gx + dx, self.gy + dy), device_id_type=MESH)

    def halo_copies(self, h):
        r = self.r
        ref = r[h["target"]]
        rows = pl.ds(TOP, h["Y"])
        out = []
        for m in h["msgs"]:
            if m[0] == "x":
                _, dx, dy, s, d, sem = m
                c = self.copy(ref.at[:, pl.ds(s, h["w"]), rows, :], ref.at[:, pl.ds(d, h["w"]), rows, :], sem, dx, 0)
                out.append((c, dx, 0))
            elif m[0] == "y":
                _, k, dy, s, d, sem = m
                out.append((self.copy(r[h["name"] + "_sy"].at[k], r[h["name"] + "_ry"].at[k], sem, 0, dy), 0, dy))
            else:
                _, k, (dx, dy), _, _, sem = m
                out.append((self.copy(r[h["name"] + "_sd"].at[k], r[h["name"] + "_rd"].at[k], sem, dx, dy), dx, dy))
        return out

    def rows_of(self, h, m, which):
        if m[0] == "y":
            start = m[3 + which]
            return m[1], "y", [(c, h["px"] + p, start + q) for c in range(h["comps"])
                               for p in range(h["X"]) for q in range(h["w"])]
        g = h["diag"]
        return m[1], "d", [(c, m[3][which] + p, m[4][which] + q) for c in range(h["comps"])
                           for p in range(g) for q in range(g)]

    def halo_start(self, h):
        ref = self.r[h["target"]]
        for m in h["msgs"]:
            if m[0] == "x":
                continue
            k, kind, rows = self.rows_of(h, m, 0)
            stage = self.r[h["name"] + "_s" + kind]
            for i, (c, p, q) in enumerate(rows):
                stage[k, i:i + 1, :] = ref[c, p, q:q + 1, :]
        for c, dx, dy in self.halo_copies(h):
            pl.when(self.exists(dx, dy))(c.start)

    def halo_wait(self, h):
        ref = self.r[h["target"]]
        copies = self.halo_copies(h)
        for c, dx, dy in copies:
            pl.when(self.exists(-dx, -dy))(c.wait_recv)
        for m in h["msgs"]:
            if m[0] == "x":
                continue
            k, kind, rows = self.rows_of(h, m, 1)
            stage = self.r[h["name"] + "_r" + kind]
            for i, (c, p, q) in enumerate(rows):
                ref[c, p, q:q + 1, :] = stage[k, i:i + 1, :]

    def halo_sent(self, h):
        for c, dx, dy in self.halo_copies(h):
            pl.when(self.exists(dx, dy))(c.wait_send)

    def win_copies(self, n):
        src, dst = self.r["S" + n], self.r["R" + n]
        return [(self.copy(src, dst.at[k], self.win[n] + k, dx, dy), dx, dy) for k, (dx, dy) in enumerate(WINDOW)]

    def win_start(self, n):
        for c, dx, dy in self.win_copies(n):
            pl.when(self.exists(dx, dy))(c.start)

    def win_wait(self, n, target):
        copies = self.win_copies(n)
        for c, dx, dy in copies:
            pl.when(self.exists(-dx, -dy))(c.wait_recv)
        ref = self.r[target]
        X2, Y2 = self.X2, self.Y2
        for k, (dx, dy) in enumerate(WINDOW + [(0, 0)]):
            for c in range(ref.shape[0]):
                for p in range(X2):
                    i = (c * X2 + p) * Y2
                    if (dx, dy) == (0, 0):
                        v = self.r["S" + n][i:i + Y2, :]
                    else:
                        v = self.r["R" + n][k, i:i + Y2, :]
                    ref[c, 4 + p - dx * X2, Y2 * (1 - dy):Y2 * (2 - dy), :] = v

    def win_sent(self, n):
        for c, dx, dy in self.win_copies(n):
            pl.when(self.exists(dx, dy))(c.wait_send)

    def coefs(self, E, K, a, b, scale):
        E, K = self.r[E], self.r[K]
        Z = E.shape[-1]
        shape = E.shape[-2:]
        R = shape[0]
        s = 1.0 / scale

        @pl.loop(a, b)
        def _(i):
            z = lax.broadcasted_iota(jnp.int32, shape, 1)
            e = E[0, i]

            def face(o):
                t = e + o
                return jnp.where(jnp.minimum(e, o) > 0.0, t * (0.5 * s), t * s)

            zp = jnp.where(z == Z - 1, 0.0, pltpu.roll(e, Z - 1, 1))
            zm = jnp.where(z == 0, 0.0, pltpu.roll(e, 1, 1))
            others = (E[0, i + 1], E[0, i - 1], pltpu.roll(e, R - 1, 0), pltpu.roll(e, 1, 0), zp, zm)
            diag = None
            for k, o in enumerate(others):
                c = face(o)
                diag = c if diag is None else diag + c
                if k == 4:
                    c = jnp.where(z == Z - 1, 0.0, c)
                if k == 5:
                    c = jnp.where(z == 0, 0.0, c)
                K[k, i] = c
            inside = e > 0.0
            K[6, i] = jnp.where(inside, WEIGHT / jnp.where(inside, diag, 1.0), 0.0)
            K[7, i] = diag

    def stencil(self, V, K, G, i, c, rows):
        R, Z = V.shape[-2:]
        n = rows.stop - rows.start
        v = V[c, i, rows, :]
        if n == R:
            yp, ym = pltpu.roll(v, R - 1, 0), pltpu.roll(v, 1, 0)
        else:
            yp, ym = V[c, i, rows.start + 1:rows.stop + 1, :], V[c, i, rows.start - 1:rows.stop - 1, :]
        acc = G[c, i, rows, :]
        parts = (V[c, i + 1, rows, :], V[c, i - 1, rows, :], yp, ym, pltpu.roll(v, Z - 1, 1), pltpu.roll(v, 1, 1))
        for k, o in enumerate(parts):
            acc = acc + K[k, i, rows, :] * o
        return v, acc

    def first(self, K, G, O, a, b):
        K, G, O = (self.r[n] for n in (K, G, O))

        @pl.loop(a, b)
        def _(i):
            w = K[6, i]
            for c in range(self.C):
                O[c, i] = w * G[c, i]

    def sweep(self, V, K, G, O, a, b, rows=None, shift=0):
        V, K, G, O = (self.r[n] for n in (V, K, G, O))
        rows = rows or slice(0, V.shape[-2])
        out_rows = rows if shift == 0 else slice(0, rows.stop - rows.start)

        @pl.loop(a, b)
        def _(i):
            for c in range(self.C):
                v, acc = self.stencil(V, K, G, i, c, rows)
                O[c, i - shift, out_rows, :] = (1.0 - WEIGHT) * v + K[6, i, rows, :] * acc

    def residual(self, V, K, G, T, px, Xc, Y):
        V, K, G, T = (self.r[n] for n in (V, K, G, T))
        rows = slice(TOP, TOP + Y)

        @pl.loop(0, Xc)
        def _(j):
            for c in range(self.C):
                total = None
                for q in range(2):
                    i = px + 2 * j + q
                    v, acc = self.stencil(V, K, G, i, c, rows)
                    d = acc - K[7, i, rows, :] * v
                    total = d if total is None else total + d
                T[pl.ds(pl.multiple_of((c * Xc + j) * Y, 8), Y), :] = 0.5 * total

    def dot(self, a, b):
        return lax.dot_general(a, b, (((1,), (0,)), ((), ())), precision=lax.Precision.HIGHEST,
                               preferred_element_type=jnp.float32)

    def pairs(self, n, m, value, fine_dim):
        r = lax.broadcasted_iota(jnp.int32, (n, m), 0)
        c = lax.broadcasted_iota(jnp.int32, (n, m), 1)
        hit = (r >> 1) == c if fine_dim == 0 else (c >> 1) == r
        return jnp.where(hit, value, 0.0).astype(jnp.float32)

    def squeeze(self, t):
        rows, Z = t.shape
        half = self.dot(t, self.pairs(Z, Z // 2, 0.5, 0))
        return self.dot(self.pairs(rows // 2, rows, 0.5, 1), half)

    def prolong(self, W, a, count, U, V, planes, coarse_of, offset):
        W, U, V = (self.r[n] for n in (W, U, V))
        C, _, Rc, Zc = W.shape
        Rf, Zf = V.shape[-2:]
        src = W[:, a:a + count].reshape(C * count * Rc, Zc)
        U[...] = self.dot(src, self.pairs(Zf, Zc, 1.0, 0).T if False else self.pairs(Zc, Zf, 1.0, 1))
        r = lax.broadcasted_iota(jnp.int32, (Rf, Rc), 0)
        c = lax.broadcasted_iota(jnp.int32, (Rf, Rc), 1)
        lift = jnp.where(((r + 2 * offset - TOP) >> 1) == c, 1.0, 0.0).astype(jnp.float32)
        for comp in range(C):
            for k in range(count):
                start = (comp * count + k) * Rc
                block = self.dot(lift, U[start:start + Rc, :])
                for p in planes:
                    if coarse_of(p) == a + k:
                        V[comp, p] = V[comp, p] + block

    def body(self, forcing, phase, out, *scratch):
        names = list(self.scratch)
        self.r = r = dict(zip(names, scratch))
        self.ssem, self.rsem, lsem = scratch[len(names):]
        self.gx, self.gy = lax.axis_index("gx"), lax.axis_index("gy")
        X, Y, Z, C = self.X, self.Y, self.Z, self.C
        X1, Y1 = self.X1, self.Y1
        block = (pl.ds(2, X), pl.ds(TOP, Y))
        load_p = pltpu.make_async_copy(phase, r["ph"], lsem.at[0])
        load_p.start()
        for n in ("E0", "F0", "V0", "E1", "F1", "V1", "E2", "F2", "A2"):
            ref = r[n]
            for c in range(ref.shape[0]):
                @pl.loop(0, ref.shape[1])
                def _(i):
                    ref[c, i] = jnp.zeros(ref.shape[2:], jnp.float32)
        for n in list(r):
            if n.startswith("h") and n[-3:] in ("_ry", "_rd") or n in ("Re2", "Rf2", "Rv2"):
                ref = r[n]
                for k in range(ref.shape[0]):
                    ref[k] = jnp.zeros(ref.shape[1:], jnp.float32)
        load_f = pltpu.make_async_copy(forcing, r["F0"].at[:, block[0], block[1], :], lsem.at[1])
        load_f.start()

        barrier = pltpu.get_barrier_semaphore()
        count = jnp.int32(0)
        for dx, dy in WINDOW:
            ok = self.exists(dx, dy)
            count = count + ok.astype(jnp.int32)

            @pl.when(ok)
            def _():
                pl.semaphore_signal(barrier, inc=1, device_id=(self.gx + dx, self.gy + dy), device_id_type=MESH)
        load_p.wait()

        @pl.loop(0, X)
        def _(i):
            ph = r["ph"][i]
            e = jnp.zeros(ph.shape, jnp.float32)
            for k, value in enumerate(VISCOSITIES):
                e = jnp.where(ph == k, jnp.float32(value), e)
            r["E0"][0, i + 2, TOP:TOP + Y, :] = e
        pl.semaphore_wait(barrier, count)
        self.halo_start(self.hE0)
        load_f.wait()
        self.halo_start(self.hF0)

        for j in range(X1):
            r["T0"][j * Y:(j + 1) * Y, :] = 0.5 * (
                r["E0"][0, 2 + 2 * j, TOP:TOP + Y, :] + r["E0"][0, 3 + 2 * j, TOP:TOP + Y, :])
        e1 = self.squeeze(r["T0"][0:X1 * Y, :])
        for j in range(X1):
            r["E1"][0, 3 + j, TOP:TOP + Y1, :] = e1[j * Y1:(j + 1) * Y1]
        self.halo_start(self.hE1)
        for j in range(self.X2):
            r["T1"][j * Y1:(j + 1) * Y1, :] = 0.5 * (
                e1[2 * j * Y1:(2 * j + 1) * Y1] + e1[(2 * j + 1) * Y1:(2 * j + 2) * Y1])
        r["Se2"][...] = self.squeeze(r["T1"][0:self.X2 * Y1, :])
        self.win_start("e2")

        self.halo_wait(self.hE0)
        self.coefs("E0", "C0", 1, X + 3, 1.0)
        self.halo_wait(self.hF0)
        self.first("C0", "F0", "A0", 1, X + 3)
        rows0 = slice(TOP, TOP + Y)
        self.sweep("A0", "C0", "F0", "V0", 2, X + 2, rows0)
        self.halo_start(self.hV0)
        self.halo_wait(self.hE1)
        self.coefs("E1", "C1", 1, X1 + 5, 4.0)
        self.win_wait("e2", "E2")
        self.coefs("E2", "C2", 1, self.X2 + 7, 16.0)
        self.halo_wait(self.hV0)
        self.residual("V0", "C0", "F0", "T0", 2, X1, Y)
        f1 = self.squeeze(r["T0"][...])
        for c in range(C):
            for j in range(X1):
                s = (c * X1 + j) * Y1
                r["F1"][c, 3 + j, TOP:TOP + Y1, :] = f1[s:s + Y1]

        self.halo_start(self.hF1)
        self.halo_wait(self.hF1)
        self.halo_start(self.hW0)
        self.first("C1", "F1", "A1", 1, X1 + 5)
        self.sweep("A1", "C1", "F1", "B1", 2, X1 + 4)
        self.residual("B1", "C1", "F1", "T1", 3, self.X2, Y1)
        r["Sf2"][...] = self.squeeze(r["T1"][...])
        self.win_start("f2")
        for c in range(C):
            for j in range(X1):
                r["V1"][c, 3 + j, TOP:TOP + Y1, :] = r["B1"][c, 3 + j, TOP:TOP + Y1, :]
        self.halo_start(self.hV1)

        self.win_wait("f2", "F2")
        p2 = self.P2
        self.first("C2", "F2", "A2", 1, p2 - 1)
        self.sweep("A2", "C2", "F2", "B2", 2, p2 - 2)
        self.sweep("B2", "C2", "F2", "A2", 3, p2 - 3)
        self.sweep("A2", "C2", "F2", "B2", 4, p2 - 4)
        for c in range(C):
            for p in range(self.X2):
                i = (c * self.X2 + p) * self.Y2
                r["Sv2"][i:i + self.Y2, :] = r["B2"][c, 4 + p, self.Y2:2 * self.Y2, :]
        self.win_start("v2")
        self.win_wait("v2", "A2")
        self.sweep("A2", "C2", "F2", "B2", 1, p2 - 1)
        self.sweep("B2", "C2", "F2", "A2", 2, p2 - 2)

        self.halo_wait(self.hV1)
        self.halo_sent(self.hV1)
        self.prolong("A2", 2, self.X2 + 4, "UZ1", "V1", range(self.P1),
                     lambda p: 4 + (p - 3) // 2, self.Y2)
        self.sweep("V1", "C1", "F1", "A1", 1, X1 + 5)
        self.sweep("A1", "C1", "F1", "B1", 2, X1 + 4)

        self.halo_wait(self.hW0)
        self.halo_sent(self.hV0)
        self.halo_sent(self.hW0)
        self.prolong("B1", 2, X1 + 2, "UZ0", "V0", range(self.P0),
                     lambda p: 3 + (p - 2) // 2, TOP)
        self.sweep("V0", "C0", "F0", "B0", 1, X + 3)
        self.sweep("B0", "C0", "F0", "O0", 2, X + 2, rows0, shift=2)
        store = pltpu.make_async_copy(r["O0"], out, lsem.at[0])
        store.start()
        for h in (self.hE0, self.hF0, self.hE1, self.hF1):
            self.halo_sent(h)
        for n in ("e2", "f2", "v2"):
            self.win_sent(n)
        store.wait()

    def __call__(self, forcing, phase):
        any_space = pl.BlockSpec(memory_space=pl.ANY)
        sems = [pltpu.SemaphoreType.DMA((self.n_sems,)), pltpu.SemaphoreType.DMA((self.n_sems,)),
                pltpu.SemaphoreType.DMA((2,))]
        return pl.pallas_call(
            self.body,
            out_shape=jax.ShapeDtypeStruct(forcing.shape, jnp.float32),
            in_specs=[any_space, any_space],
            out_specs=any_space,
            scratch_shapes=list(self.scratch.values()) + sems,
            compiler_params=pltpu.CompilerParams(
                collective_id=0, has_side_effects=True, vmem_limit_bytes=60 * 1024 * 1024),
            name="vcycle",
        )(forcing, phase)


def solution(mesh):
    grid = (mesh.shape["gx"], mesh.shape["gy"])

    def per_device(forcing, phase_ids):
        return Kernel(phase_ids.shape, forcing.shape[0], grid)(forcing, phase_ids)

    return jax.shard_map(
        per_device,
        mesh=mesh,
        in_specs=(P(None, "gx", "gy", None), P("gx", "gy", None)),
        out_specs=P(None, "gx", "gy", None),
        check_vma=False,
    )
```

```python
import functools

import jax
import jax.numpy as jnp
from jax import lax
from jax.experimental import pallas as pl
from jax.experimental.pallas import tpu as pltpu
from jax.sharding import PartitionSpec as P

COARSE_SWEEPS = 6
VISCOSITIES = (0.2, 0.6, 1.5, 4.0)
WEIGHT = 2.0 / 3.0
MESH = pl.DeviceIdType.MESH
WINDOW = [(dx, dy) for dx in range(-2, 3) for dy in range(-1, 2) if (dx, dy) != (0, 0)]
TOP = 8


def up8(n):
    return -(-n // 8) * 8


def side_slices(step, first, length, lo, hi):
    if step > 0:
        return (first + length - hi, first - hi)
    return (first + lo - 1, first + length + lo - 1)


class Kernel:
    def __init__(self, sizes, comps, grid):
        self.X, self.Y, self.Z = sizes
        self.C = comps
        self.grid = grid
        self.scratch = {}
        self.n_sems = 0
        self.plan()

    def buf(self, name, shape, dtype=jnp.float32):
        self.scratch[name] = pltpu.VMEM(tuple(shape), dtype)

    def halo(self, name, target, comps, px, X, Y, Z, lo, hi, diag, base=0):
        w = hi - lo + 1
        msgs = []
        for dx in (1, -1):
            s, d = side_slices(dx, px, X, lo, hi)
            msgs.append(("x", dx, 0, s, d, self.n_sems))
            self.n_sems += 1
        n = comps * X * w
        self.buf(name + "_sy", (2, up8(n), Z))
        self.buf(name + "_ry", (2, up8(n), Z))
        for k, dy in enumerate((1, -1)):
            s, d = side_slices(dy, TOP, Y, lo, hi)
            msgs.append(("y", k, dy, s, d, self.n_sems))
            self.n_sems += 1
        if diag:
            n = comps * len(diag)
            self.buf(name + "_sd", (4, up8(n), Z))
            self.buf(name + "_rd", (4, up8(n), Z))
            for k, (dx, dy) in enumerate([(1, 1), (1, -1), (-1, 1), (-1, -1)]):
                cells = [[], []]
                for a, b in diag:
                    sx, tx = side_slices(dx, px, X, a, a)
                    sy, ty = side_slices(dy, TOP, Y, b, b)
                    cells[0].append((sx, sy))
                    cells[1].append((tx, ty))
                msgs.append(("d", k, (dx, dy), cells[0], cells[1], self.n_sems))
                self.n_sems += 1
        return dict(name=name, base=base, target=target, comps=comps, px=px, X=X, Y=Y, w=w, diag=diag, msgs=msgs)

    def plan(self):
        X, Y, Z, C = self.X, self.Y, self.Z, self.C
        self.P0, self.R0 = X + 4, Y + 16
        self.X1, self.Y1, self.Z1 = X // 2, Y // 2, Z // 2
        self.P1, self.R1 = self.X1 + 6, self.Y1 + 16
        self.X2, self.Y2, self.Z2 = X // 4, Y // 4, Z // 4
        self.P2, self.R2 = self.X2 + 8, up8(self.Y2 * 3)
        b = self.buf
        b("ph", (X, Y, Z), jnp.int32)
        b("E0", (1, self.P0, self.R0, Z))
        b("C0", (8, self.P0, self.R0, Z))
        for n in ("F0", "A0", "V0", "B0"):
            b(n, (C, self.P0, self.R0, Z))
        b("O0", (C, X, Y, Z))
        b("T0", (C * self.X1 * Y, Z))
        b("E1", (1, self.P1, self.R1, self.Z1))
        b("C1", (8, self.P1, self.R1, self.Z1))
        for n in ("F1", "A1", "V1", "B1"):
            b(n, (C, self.P1, self.R1, self.Z1))
        b("T1", (C * self.X2 * self.Y1, self.Z1))
        b("E2", (1, self.P2, self.R2, self.Z2))
        b("C2", (8, self.P2, self.R2, self.Z2))
        for n in ("F2", "A2", "B2"):
            b(n, (C, self.P2, self.R2, self.Z2))
        blk = self.X2 * self.Y2
        for n, c in (("e2", 1), ("f2", C), ("v2", C)):
            b("S" + n, (c * blk, self.Z2))
            b("R" + n, (len(WINDOW), c * blk, self.Z2))
        b("UZ1", (self.R2 * C * (self.X2 + 4), self.Z1))
        b("UZ0", (self.R1 * C * (self.X1 + 2), self.Z))
        reach = [(1, 1), (1, 2), (2, 1), (1, 3), (2, 2), (3, 1)]
        self.hE0 = self.halo("hE0", "E0", 1, 2, X, Y, Z, 1, 2, [(1, 1)])
        self.hF0 = self.halo("hF0", "F0", C, 2, X, Y, Z, 1, 1, [])
        self.hV0 = self.halo("hV0", "V0", C, 2, X, Y, Z, 1, 1, [])
        self.hW0 = [self.halo("hW%d" % c, "V0", 1, 2, X, Y, Z, 2, 2, [(1, 1)], c) for c in range(C)]
        self.hE1 = self.halo("hE1", "E1", 1, 3, self.X1, self.Y1, self.Z1, 1, 3, reach)
        self.hF1 = self.halo("hF1", "F1", C, 3, self.X1, self.Y1, self.Z1, 1, 2, reach[:3])
        self.hV1 = self.halo("hV1", "V1", C, 3, self.X1, self.Y1, self.Z1, 2, 3, reach[1:])
        self.win = {}
        for n in ("e2", "f2", "v2"):
            self.win[n] = self.n_sems
            self.n_sems += len(WINDOW)

    def exists(self, dx, dy):
        ok = None
        for step, me, size in ((dx, self.gx, self.grid[0]), (dy, self.gy, self.grid[1])):
            if step:
                t = (me + step >= 0) & (me + step < size)
                ok = t if ok is None else ok & t
        return ok

    def copy(self, src, dst, sem, dx, dy):
        return pltpu.make_async_remote_copy(
            src_ref=src, dst_ref=dst, send_sem=self.ssem.at[sem], recv_sem=self.rsem.at[sem],
            device_id=(self.gx + dx, self.gy + dy), device_id_type=MESH)

    def halo_copies(self, h, kinds="xyd"):
        r = self.r
        ref = r[h["target"]]
        rows = pl.ds(TOP, h["Y"])
        out = []
        for m in h["msgs"]:
            if m[0] not in kinds:
                continue
            if m[0] == "x":
                _, dx, dy, s, d, sem = m
                comps = pl.ds(h["base"], h["comps"])
                c = self.copy(ref.at[comps, pl.ds(s, h["w"]), rows, :], ref.at[comps, pl.ds(d, h["w"]), rows, :],
                              sem, dx, 0)
                out.append((c, dx, 0))
            elif m[0] == "y":
                _, k, dy, s, d, sem = m
                out.append((self.copy(r[h["name"] + "_sy"].at[k], r[h["name"] + "_ry"].at[k], sem, 0, dy), 0, dy))
            else:
                _, k, (dx, dy), _, _, sem = m
                out.append((self.copy(r[h["name"] + "_sd"].at[k], r[h["name"] + "_rd"].at[k], sem, dx, dy), dx, dy))
        return out

    def rows_of(self, h, m, which):
        if m[0] == "y":
            start = m[3 + which]
            return m[1], "y", [(c + h["base"], h["px"] + p, start + q) for c in range(h["comps"])
                               for p in range(h["X"]) for q in range(h["w"])]
        return m[1], "d", [(c + h["base"], p, q) for c in range(h["comps"]) for p, q in m[3 + which]]

    def halo_start(self, h, kinds="xyd"):
        ref = self.r[h["target"]]
        for m in h["msgs"]:
            if m[0] == "x" or m[0] not in kinds:
                continue
            k, kind, rows = self.rows_of(h, m, 0)
            stage = self.r[h["name"] + "_s" + kind]
            for i, (c, p, q) in enumerate(rows):
                stage[k, i:i + 1, :] = ref[c, p, q:q + 1, :]
        for c, dx, dy in self.halo_copies(h, kinds):
            pl.when(self.exists(dx, dy))(c.start)

    def halo_wait(self, h, kinds="xyd"):
        ref = self.r[h["target"]]
        for c, dx, dy in self.halo_copies(h, kinds):
            pl.when(self.exists(-dx, -dy))(c.wait_recv)
        for m in h["msgs"]:
            if m[0] == "x" or m[0] not in kinds:
                continue
            k, kind, rows = self.rows_of(h, m, 1)
            stage = self.r[h["name"] + "_r" + kind]
            for i, (c, p, q) in enumerate(rows):
                ref[c, p, q:q + 1, :] = stage[k, i:i + 1, :]

    def halo_sent(self, h):
        for c, dx, dy in self.halo_copies(h):
            pl.when(self.exists(dx, dy))(c.wait_send)

    def win_copies(self, n):
        src, dst = self.r["S" + n], self.r["R" + n]
        return [(self.copy(src, dst.at[k], self.win[n] + k, dx, dy), dx, dy) for k, (dx, dy) in enumerate(WINDOW)]

    def win_start(self, n):
        for c, dx, dy in self.win_copies(n):
            pl.when(self.exists(dx, dy))(c.start)

    def win_wait(self, n, target):
        copies = self.win_copies(n)
        for c, dx, dy in copies:
            pl.when(self.exists(-dx, -dy))(c.wait_recv)
        ref = self.r[target]
        X2, Y2 = self.X2, self.Y2
        for k, (dx, dy) in enumerate(WINDOW + [(0, 0)]):
            for c in range(ref.shape[0]):
                for p in range(X2):
                    i = (c * X2 + p) * Y2
                    if (dx, dy) == (0, 0):
                        v = self.r["S" + n][i:i + Y2, :]
                    else:
                        v = self.r["R" + n][k, i:i + Y2, :]
                    ref[c, 4 + p - dx * X2, Y2 * (1 - dy):Y2 * (2 - dy), :] = v

    def win_sent(self, n):
        for c, dx, dy in self.win_copies(n):
            pl.when(self.exists(dx, dy))(c.wait_send)

    def coefs(self, E, K, a, b, scale):
        E, K = self.r[E], self.r[K]
        Z = E.shape[-1]
        shape = E.shape[-2:]
        R = shape[0]
        s = 1.0 / scale

        @pl.loop(a, b)
        def _(i):
            z = lax.broadcasted_iota(jnp.int32, shape, 1)
            e = E[0, i]

            def face(o):
                t = e + o
                return jnp.where(jnp.minimum(e, o) > 0.0, t * (0.5 * s), t * s)

            zp = jnp.where(z == Z - 1, 0.0, pltpu.roll(e, Z - 1, 1))
            zm = jnp.where(z == 0, 0.0, pltpu.roll(e, 1, 1))
            others = (E[0, i + 1], E[0, i - 1], pltpu.roll(e, R - 1, 0), pltpu.roll(e, 1, 0), zp, zm)
            diag = None
            for k, o in enumerate(others):
                c = face(o)
                diag = c if diag is None else diag + c
                if k == 4:
                    c = jnp.where(z == Z - 1, 0.0, c)
                if k == 5:
                    c = jnp.where(z == 0, 0.0, c)
                K[k, i] = c
            inside = e > 0.0
            K[6, i] = jnp.where(inside, WEIGHT / jnp.where(inside, diag, 1.0), 0.0)
            K[7, i] = diag

    def stencil(self, V, K, G, i, c, rows):
        R, Z = V.shape[-2:]
        n = rows.stop - rows.start
        v = V[c, i, rows, :]
        if n == R:
            yp, ym = pltpu.roll(v, R - 1, 0), pltpu.roll(v, 1, 0)
        else:
            yp, ym = V[c, i, rows.start + 1:rows.stop + 1, :], V[c, i, rows.start - 1:rows.stop - 1, :]
        acc = G[c, i, rows, :]
        parts = (V[c, i + 1, rows, :], V[c, i - 1, rows, :], yp, ym, pltpu.roll(v, Z - 1, 1), pltpu.roll(v, 1, 1))
        for k, o in enumerate(parts):
            acc = acc + K[k, i, rows, :] * o
        return v, acc

    def first(self, K, G, O, a, b):
        K, G, O = (self.r[n] for n in (K, G, O))

        @pl.loop(a, b)
        def _(i):
            w = K[6, i]
            for c in range(self.C):
                O[c, i] = w * G[c, i]

    def sweep(self, V, K, G, O, a, b, rows=None, shift=0):
        V, K, G, O = (self.r[n] for n in (V, K, G, O))
        rows = rows or slice(0, V.shape[-2])
        out_rows = rows if shift == 0 else slice(0, rows.stop - rows.start)

        @pl.loop(a, b)
        def _(i):
            for c in range(self.C):
                v, acc = self.stencil(V, K, G, i, c, rows)
                O[c, i - shift, out_rows, :] = (1.0 - WEIGHT) * v + K[6, i, rows, :] * acc

    def residual(self, V, K, G, T, px, Xc, Y, a=0, b=None):
        V, K, G, T = (self.r[n] for n in (V, K, G, T))
        rows = slice(TOP, TOP + Y)

        @pl.loop(a, Xc if b is None else b)
        def _(j):
            for c in range(self.C):
                total = None
                for q in range(2):
                    i = px + 2 * j + q
                    v, acc = self.stencil(V, K, G, i, c, rows)
                    d = acc - K[7, i, rows, :] * v
                    total = d if total is None else total + d
                T[pl.ds(pl.multiple_of((c * Xc + j) * Y, 8), Y), :] = 0.5 * total

    def dot(self, a, b):
        return lax.dot_general(a, b, (((1,), (0,)), ((), ())), precision=lax.Precision.HIGHEST,
                               preferred_element_type=jnp.float32)

    def pairs(self, n, m, value, fine_dim):
        r = lax.broadcasted_iota(jnp.int32, (n, m), 0)
        c = lax.broadcasted_iota(jnp.int32, (n, m), 1)
        hit = (r >> 1) == c if fine_dim == 0 else (c >> 1) == r
        return jnp.where(hit, value, 0.0).astype(jnp.float32)

    def squeeze(self, t):
        rows, Z = t.shape
        half = self.dot(t, self.pairs(Z, Z // 2, 0.5, 0))
        return self.dot(self.pairs(rows // 2, rows, 0.5, 1), half)

    def prolong(self, W, a, count, U, V, planes, coarse_of, offset):
        W, U, V = (self.r[n] for n in (W, U, V))
        C, _, Rc, Zc = W.shape
        Rf, Zf = V.shape[-2:]
        src = W[:, a:a + count].reshape(C * count * Rc, Zc)
        U[...] = self.dot(src, self.pairs(Zf, Zc, 1.0, 0).T if False else self.pairs(Zc, Zf, 1.0, 1))
        r = lax.broadcasted_iota(jnp.int32, (Rf, Rc), 0)
        c = lax.broadcasted_iota(jnp.int32, (Rf, Rc), 1)
        lift = jnp.where(((r + 2 * offset - TOP) >> 1) == c, 1.0, 0.0).astype(jnp.float32)
        for comp in range(C):
            for k in range(count):
                start = (comp * count + k) * Rc
                block = self.dot(lift, U[start:start + Rc, :])
                for p in planes:
                    if coarse_of(p) == a + k:
                        V[comp, p] = V[comp, p] + block

    def body(self, forcing, phase, out, *scratch):
        names = list(self.scratch)
        self.r = r = dict(zip(names, scratch))
        self.ssem, self.rsem, lsem = scratch[len(names):]
        self.gx, self.gy = lax.axis_index("gx"), lax.axis_index("gy")
        X, Y, Z, C = self.X, self.Y, self.Z, self.C
        X1, Y1 = self.X1, self.Y1
        block = (pl.ds(2, X), pl.ds(TOP, Y))
        load_p = pltpu.make_async_copy(phase, r["ph"], lsem.at[0])
        load_p.start()
        for n in ("E0", "F0", "V0", "E1", "F1", "V1", "E2", "F2", "A2"):
            ref = r[n]
            for c in range(ref.shape[0]):
                @pl.loop(0, ref.shape[1])
                def _(i):
                    ref[c, i] = jnp.zeros(ref.shape[2:], jnp.float32)
        for n in list(r):
            if n.startswith("h") and n[-3:] in ("_ry", "_rd") or n in ("Re2", "Rf2", "Rv2"):
                ref = r[n]
                for k in range(ref.shape[0]):
                    ref[k] = jnp.zeros(ref.shape[1:], jnp.float32)
        load_f = pltpu.make_async_copy(forcing, r["F0"].at[:, block[0], block[1], :], lsem.at[1])
        load_f.start()

        barrier = pltpu.get_barrier_semaphore()
        count = jnp.int32(0)
        for dx, dy in WINDOW:
            ok = self.exists(dx, dy)
            count = count + ok.astype(jnp.int32)

            @pl.when(ok)
            def _():
                pl.semaphore_signal(barrier, inc=1, device_id=(self.gx + dx, self.gy + dy), device_id_type=MESH)
        load_p.wait()

        @pl.loop(0, X)
        def _(i):
            ph = r["ph"][i]
            e = jnp.zeros(ph.shape, jnp.float32)
            for k, value in enumerate(VISCOSITIES):
                e = jnp.where(ph == k, jnp.float32(value), e)
            r["E0"][0, i + 2, TOP:TOP + Y, :] = e
        pl.semaphore_wait(barrier, count)
        self.halo_start(self.hE0)
        load_f.wait()
        self.halo_start(self.hF0)

        for j in range(X1):
            r["T0"][j * Y:(j + 1) * Y, :] = 0.5 * (
                r["E0"][0, 2 + 2 * j, TOP:TOP + Y, :] + r["E0"][0, 3 + 2 * j, TOP:TOP + Y, :])
        e1 = self.squeeze(r["T0"][0:X1 * Y, :])
        for j in range(X1):
            r["E1"][0, 3 + j, TOP:TOP + Y1, :] = e1[j * Y1:(j + 1) * Y1]
        self.halo_start(self.hE1)
        for j in range(self.X2):
            r["T1"][j * Y1:(j + 1) * Y1, :] = 0.5 * (
                e1[2 * j * Y1:(2 * j + 1) * Y1] + e1[(2 * j + 1) * Y1:(2 * j + 2) * Y1])
        r["Se2"][...] = self.squeeze(r["T1"][0:self.X2 * Y1, :])
        self.win_start("e2")

        self.halo_wait(self.hE0, "y")
        self.coefs("E0", "C0", 3, X + 1, 1.0)
        self.halo_wait(self.hE0, "xd")
        self.coefs("E0", "C0", 1, 3, 1.0)
        self.coefs("E0", "C0", X + 1, X + 3, 1.0)
        self.halo_wait(self.hF0)
        self.first("C0", "F0", "A0", 1, X + 3)
        rows0 = slice(TOP, TOP + Y)
        self.sweep("A0", "C0", "F0", "V0", 2, 3, rows0)
        self.sweep("A0", "C0", "F0", "V0", X + 1, X + 2, rows0)
        self.halo_start(self.hV0, "x")
        self.sweep("A0", "C0", "F0", "V0", 3, X + 1, rows0)
        self.halo_start(self.hV0, "yd")
        self.halo_wait(self.hE1)
        self.coefs("E1", "C1", 1, X1 + 5, 4.0)
        self.win_wait("e2", "E2")
        self.coefs("E2", "C2", 1, self.X2 + 7, 16.0)
        self.halo_wait(self.hV0, "y")
        self.residual("V0", "C0", "F0", "T0", 2, X1, Y, 1, X1 - 1)
        self.halo_wait(self.hV0, "x")
        self.residual("V0", "C0", "F0", "T0", 2, X1, Y, 0, 1)
        self.residual("V0", "C0", "F0", "T0", 2, X1, Y, X1 - 1, X1)
        f1 = self.squeeze(r["T0"][...])
        for c in range(C):
            for j in range(X1):
                s = (c * X1 + j) * Y1
                r["F1"][c, 3 + j, TOP:TOP + Y1, :] = f1[s:s + Y1]

        self.halo_start(self.hF1)
        self.halo_wait(self.hF1)
        self.first("C1", "F1", "A1", 1, X1 + 5)
        self.sweep("A1", "C1", "F1", "B1", 2, X1 + 4)
        self.residual("B1", "C1", "F1", "T1", 3, self.X2, Y1)
        r["Sf2"][...] = self.squeeze(r["T1"][...])
        self.win_start("f2")
        for c in range(C):
            for j in range(X1):
                r["V1"][c, 3 + j, TOP:TOP + Y1, :] = r["B1"][c, 3 + j, TOP:TOP + Y1, :]
            for dx in (2, X1 + 3):
                r["V1"][c, dx, TOP - 1:TOP + Y1 + 1, :] = r["B1"][c, dx, TOP - 1:TOP + Y1 + 1, :]
            for j in range(X1):
                for q in (TOP - 1, TOP + Y1):
                    r["V1"][c, 3 + j, q:q + 1, :] = r["B1"][c, 3 + j, q:q + 1, :]
        self.halo_start(self.hV1)

        self.win_wait("f2", "F2")
        p2 = self.P2
        self.first("C2", "F2", "A2", 1, p2 - 1)
        self.sweep("A2", "C2", "F2", "B2", 2, p2 - 2)
        self.sweep("B2", "C2", "F2", "A2", 3, p2 - 3)
        self.sweep("A2", "C2", "F2", "B2", 4, p2 - 4)
        for c in range(C):
            for p in range(self.X2):
                i = (c * self.X2 + p) * self.Y2
                r["Sv2"][i:i + self.Y2, :] = r["B2"][c, 4 + p, self.Y2:2 * self.Y2, :]
        self.win_start("v2")
        for h in self.hW0:
            self.halo_start(h)
        self.win_wait("v2", "A2")
        self.sweep("A2", "C2", "F2", "B2", 1, p2 - 1)
        self.sweep("B2", "C2", "F2", "A2", 2, p2 - 2)

        self.halo_wait(self.hV1)
        self.halo_sent(self.hV1)
        self.prolong("A2", 2, self.X2 + 4, "UZ1", "V1", range(self.P1),
                     lambda p: 4 + (p - 3) // 2, self.Y2)
        self.sweep("V1", "C1", "F1", "A1", 1, X1 + 5)
        self.sweep("A1", "C1", "F1", "B1", 2, X1 + 4)

        for h in self.hW0:
            self.halo_wait(h)
            self.halo_sent(h)
        self.halo_sent(self.hV0)
        self.prolong("B1", 2, X1 + 2, "UZ0", "V0", range(self.P0),
                     lambda p: 3 + (p - 2) // 2, TOP)
        self.sweep("V0", "C0", "F0", "B0", 1, X + 3)
        self.sweep("B0", "C0", "F0", "O0", 2, X + 2, rows0, shift=2)
        store = pltpu.make_async_copy(r["O0"], out, lsem.at[0])
        store.start()
        for h in (self.hE0, self.hF0, self.hE1, self.hF1):
            self.halo_sent(h)
        for n in ("e2", "f2", "v2"):
            self.win_sent(n)
        store.wait()

    def __call__(self, forcing, phase):
        any_space = pl.BlockSpec(memory_space=pl.ANY)
        sems = [pltpu.SemaphoreType.DMA((self.n_sems,)), pltpu.SemaphoreType.DMA((self.n_sems,)),
                pltpu.SemaphoreType.DMA((2,))]
        return pl.pallas_call(
            self.body,
            out_shape=jax.ShapeDtypeStruct(forcing.shape, jnp.float32),
            in_specs=[any_space, any_space],
            out_specs=any_space,
            scratch_shapes=list(self.scratch.values()) + sems,
            compiler_params=pltpu.CompilerParams(
                collective_id=0, has_side_effects=True, vmem_limit_bytes=60 * 1024 * 1024),
            name="vcycle",
        )(forcing, phase)


def solution(mesh):
    grid = (mesh.shape["gx"], mesh.shape["gy"])

    def per_device(forcing, phase_ids):
        return Kernel(phase_ids.shape, forcing.shape[0], grid)(forcing, phase_ids)

    return jax.shard_map(
        per_device,
        mesh=mesh,
        in_specs=(P(None, "gx", "gy", None), P("gx", "gy", None)),
        out_specs=P(None, "gx", "gy", None),
        check_vma=False,
    )
```

```python
import functools

import jax
import jax.numpy as jnp
from jax import lax
from jax.experimental import pallas as pl
from jax.experimental.pallas import tpu as pltpu
from jax.sharding import PartitionSpec as P

COARSE_SWEEPS = 6
VISCOSITIES = (0.2, 0.6, 1.5, 4.0)
WEIGHT = 2.0 / 3.0
MESH = pl.DeviceIdType.MESH
WINDOW = [(dx, dy) for dx in range(-2, 3) for dy in range(-1, 2) if (dx, dy) != (0, 0)]
TOP = 0


def up8(n):
    return -(-n // 8) * 8


def side_slices(step, first, length, lo, hi):
    if step > 0:
        return (first + length - hi, first - hi)
    return (first + lo - 1, first + length + lo - 1)


class Kernel:
    def __init__(self, sizes, comps, grid):
        self.X, self.Y, self.Z = sizes
        self.C = comps
        self.grid = grid
        self.scratch = {}
        self.n_sems = 0
        self.plan()

    def buf(self, name, shape, dtype=jnp.float32):
        self.scratch[name] = pltpu.VMEM(tuple(shape), dtype)

    def halo(self, name, target, comps, px, X, Y, Z, lo, hi, diag, base=0):
        w = hi - lo + 1
        msgs = []
        for dx in (1, -1):
            s, d = side_slices(dx, px, X, lo, hi)
            msgs.append(("x", dx, 0, s, d, self.n_sems))
            self.n_sems += 1
        n = comps * X * w
        self.buf(name + "_sy", (2, up8(n), Z))
        self.buf(name + "_ry", (2, up8(n), Z))
        for k, dy in enumerate((1, -1)):
            s, d = side_slices(dy, TOP, Y, lo, hi)
            d %= Y + 8
            msgs.append(("y", k, dy, s, d, self.n_sems))
            self.n_sems += 1
        if diag:
            n = comps * len(diag)
            self.buf(name + "_sd", (4, n, 1, Z))
            self.buf(name + "_rd", (4, n, 1, Z))
            for k, (dx, dy) in enumerate([(1, 1), (1, -1), (-1, 1), (-1, -1)]):
                cells = [[], []]
                for a, b in diag:
                    sx, tx = side_slices(dx, px, X, a, a)
                    sy, ty = side_slices(dy, TOP, Y, b, b)
                    cells[0].append((sx, sy))
                    cells[1].append((tx, ty % (Y + 8)))
                msgs.append(("d", k, (dx, dy), cells[0], cells[1], self.n_sems))
                self.n_sems += 1
        return dict(name=name, base=base, target=target, comps=comps, px=px, X=X, Y=Y, w=w, diag=diag, msgs=msgs)

    def plan(self):
        X, Y, Z, C = self.X, self.Y, self.Z, self.C
        self.P0, self.R0 = X + 4, Y + 8
        self.X1, self.Y1, self.Z1 = X // 2, Y // 2, Z // 2
        self.P1, self.R1 = self.X1 + 6, self.Y1 + 8
        self.X2, self.Y2, self.Z2 = X // 4, Y // 4, Z // 4
        self.P2, self.R2 = self.X2 + 8, up8(self.Y2 * 3)
        b = self.buf
        b("ph", (X, Y, Z), jnp.int32)
        b("E0", (1, self.P0, self.R0, Z))
        b("C0", (8, self.P0, self.R0, Z))
        for n in ("F0", "A0", "V0", "B0"):
            b(n, (C, self.P0, self.R0, Z))
        b("O0", (C, X, Y, Z))
        b("T0", (C * self.X1 * Y, Z))
        b("E1", (1, self.P1, self.R1, self.Z1))
        b("C1", (8, self.P1, self.R1, self.Z1))
        for n in ("F1", "A1", "V1", "B1"):
            b(n, (C, self.P1, self.R1, self.Z1))
        b("T1", (C * self.X2 * self.Y1, self.Z1))
        b("E2", (1, self.P2, self.R2, self.Z2))
        b("C2", (8, self.P2, self.R2, self.Z2))
        for n in ("F2", "A2", "B2"):
            b(n, (C, self.P2, self.R2, self.Z2))
        blk = self.X2 * self.Y2
        for n, c in (("e2", 1), ("f2", C), ("v2", C)):
            b("S" + n, (c * blk, self.Z2))
            b("R" + n, (len(WINDOW), c * blk, self.Z2))
        b("UZ1", (self.R2 * C * (self.X2 + 4), self.Z1))
        b("UZ0", (self.R1 * C * (self.X1 + 2), self.Z))
        reach = [(1, 1), (1, 2), (2, 1), (1, 3), (2, 2), (3, 1)]
        self.hE0 = self.halo("hE0", "E0", 1, 2, X, Y, Z, 1, 2, [(1, 1)])
        self.hF0 = self.halo("hF0", "F0", C, 2, X, Y, Z, 1, 1, [])
        self.hV0 = self.halo("hV0", "V0", C, 2, X, Y, Z, 1, 1, [])
        self.hW0 = [self.halo("hW%d" % c, "V0", 1, 2, X, Y, Z, 2, 2, [(1, 1)], c) for c in range(C)]
        self.hE1 = self.halo("hE1", "E1", 1, 3, self.X1, self.Y1, self.Z1, 1, 3, reach)
        self.hF1 = self.halo("hF1", "F1", C, 3, self.X1, self.Y1, self.Z1, 1, 2, reach[:3])
        self.hV1 = self.halo("hV1", "V1", C, 3, self.X1, self.Y1, self.Z1, 2, 3, reach[1:])
        self.win = {}
        for n in ("e2", "f2", "v2"):
            self.win[n] = self.n_sems
            self.n_sems += len(WINDOW)

    def exists(self, dx, dy):
        ok = None
        for step, me, size in ((dx, self.gx, self.grid[0]), (dy, self.gy, self.grid[1])):
            if step:
                t = (me + step >= 0) & (me + step < size)
                ok = t if ok is None else ok & t
        return ok

    def copy(self, src, dst, sem, dx, dy):
        return pltpu.make_async_remote_copy(
            src_ref=src, dst_ref=dst, send_sem=self.ssem.at[sem], recv_sem=self.rsem.at[sem],
            device_id=(self.gx + dx, self.gy + dy), device_id_type=MESH)

    def halo_copies(self, h, kinds="xyd"):
        r = self.r
        ref = r[h["target"]]
        rows = pl.ds(TOP, h["Y"])
        out = []
        for m in h["msgs"]:
            if m[0] not in kinds:
                continue
            if m[0] == "x":
                _, dx, dy, s, d, sem = m
                comps = pl.ds(h["base"], h["comps"])
                c = self.copy(ref.at[comps, pl.ds(s, h["w"]), rows, :], ref.at[comps, pl.ds(d, h["w"]), rows, :],
                              sem, dx, 0)
                out.append((c, dx, 0))
            elif m[0] == "y":
                _, k, dy, s, d, sem = m
                out.append((self.copy(r[h["name"] + "_sy"].at[k], r[h["name"] + "_ry"].at[k], sem, 0, dy), 0, dy))
            else:
                _, k, (dx, dy), _, _, sem = m
                out.append((self.copy(r[h["name"] + "_sd"].at[k], r[h["name"] + "_rd"].at[k], sem, dx, dy), dx, dy))
        return out

    def rows_of(self, h, m, which):
        if m[0] == "y":
            start = m[3 + which]
            return m[1], "y", [(c + h["base"], h["px"] + p, start + q) for c in range(h["comps"])
                               for p in range(h["X"]) for q in range(h["w"])]
        return m[1], "d", [(c + h["base"], p, q) for c in range(h["comps"]) for p, q in m[3 + which]]

    def halo_start(self, h, kinds="xyd"):
        ref = self.r[h["target"]]
        for m in h["msgs"]:
            if m[0] == "x" or m[0] not in kinds:
                continue
            k, kind, rows = self.rows_of(h, m, 0)
            stage = self.r[h["name"] + "_s" + kind]
            for i, (c, p, q) in enumerate(rows):
                row = ref[c, p, q:q + 1, :]
                if kind == "d":
                    stage[k, i] = row
                else:
                    stage[k, i:i + 1, :] = row
        for c, dx, dy in self.halo_copies(h, kinds):
            pl.when(self.exists(dx, dy))(c.start)

    def halo_wait(self, h, kinds="xyd"):
        ref = self.r[h["target"]]
        for c, dx, dy in self.halo_copies(h, kinds):
            pl.when(self.exists(-dx, -dy))(c.wait_recv)
        for m in h["msgs"]:
            if m[0] == "x" or m[0] not in kinds:
                continue
            k, kind, rows = self.rows_of(h, m, 1)
            stage = self.r[h["name"] + "_r" + kind]
            for i, (c, p, q) in enumerate(rows):
                ref[c, p, q:q + 1, :] = stage[k, i] if kind == "d" else stage[k, i:i + 1, :]

    def halo_sent(self, h):
        for c, dx, dy in self.halo_copies(h):
            pl.when(self.exists(dx, dy))(c.wait_send)

    def win_copies(self, n):
        src, dst = self.r["S" + n], self.r["R" + n]
        return [(self.copy(src, dst.at[k], self.win[n] + k, dx, dy), dx, dy) for k, (dx, dy) in enumerate(WINDOW)]

    def win_start(self, n):
        for c, dx, dy in self.win_copies(n):
            pl.when(self.exists(dx, dy))(c.start)

    def win_wait(self, n, target):
        copies = self.win_copies(n)
        for c, dx, dy in copies:
            pl.when(self.exists(-dx, -dy))(c.wait_recv)
        ref = self.r[target]
        X2, Y2 = self.X2, self.Y2
        for k, (dx, dy) in enumerate(WINDOW + [(0, 0)]):
            for c in range(ref.shape[0]):
                for p in range(X2):
                    i = (c * X2 + p) * Y2
                    if (dx, dy) == (0, 0):
                        v = self.r["S" + n][i:i + Y2, :]
                    else:
                        v = self.r["R" + n][k, i:i + Y2, :]
                    ref[c, 4 + p - dx * X2, Y2 * (1 - dy):Y2 * (2 - dy), :] = v

    def win_sent(self, n):
        for c, dx, dy in self.win_copies(n):
            pl.when(self.exists(dx, dy))(c.wait_send)

    def coefs(self, E, K, a, b, scale):
        E, K = self.r[E], self.r[K]
        Z = E.shape[-1]
        shape = E.shape[-2:]
        R = shape[0]
        s = 1.0 / scale

        @pl.loop(a, b)
        def _(i):
            z = lax.broadcasted_iota(jnp.int32, shape, 1)
            e = E[0, i]

            def face(o):
                t = e + o
                return jnp.where(jnp.minimum(e, o) > 0.0, t * (0.5 * s), t * s)

            zp = jnp.where(z == Z - 1, 0.0, pltpu.roll(e, Z - 1, 1))
            zm = jnp.where(z == 0, 0.0, pltpu.roll(e, 1, 1))
            others = (E[0, i + 1], E[0, i - 1], pltpu.roll(e, R - 1, 0), pltpu.roll(e, 1, 0), zp, zm)
            diag = None
            for k, o in enumerate(others):
                c = face(o)
                diag = c if diag is None else diag + c
                if k == 4:
                    c = jnp.where(z == Z - 1, 0.0, c)
                if k == 5:
                    c = jnp.where(z == 0, 0.0, c)
                K[k, i] = c
            inside = e > 0.0
            K[6, i] = jnp.where(inside, WEIGHT / jnp.where(inside, diag, 1.0), 0.0)
            K[7, i] = diag

    def stencil(self, V, K, G, i, c, rows):
        R, Z = V.shape[-2:]
        n = rows.stop - rows.start
        v = V[c, i, rows, :]
        if n == R:
            yp, ym = pltpu.roll(v, R - 1, 0), pltpu.roll(v, 1, 0)
        else:
            yp, ym = V[c, i, 1:n + 1, :], pltpu.roll(V[c, i], 1, 0)[:n]
        acc = G[c, i, rows, :]
        parts = (V[c, i + 1, rows, :], V[c, i - 1, rows, :], yp, ym, pltpu.roll(v, Z - 1, 1), pltpu.roll(v, 1, 1))
        for k, o in enumerate(parts):
            acc = acc + K[k, i, rows, :] * o
        return v, acc

    def first(self, K, G, O, a, b):
        K, G, O = (self.r[n] for n in (K, G, O))

        @pl.loop(a, b)
        def _(i):
            w = K[6, i]
            for c in range(self.C):
                O[c, i] = w * G[c, i]

    def sweep(self, V, K, G, O, a, b, rows=None, shift=0):
        V, K, G, O = (self.r[n] for n in (V, K, G, O))
        rows = rows or slice(0, V.shape[-2])
        out_rows = rows if shift == 0 else slice(0, rows.stop - rows.start)

        @pl.loop(a, b)
        def _(i):
            for c in range(self.C):
                v, acc = self.stencil(V, K, G, i, c, rows)
                O[c, i - shift, out_rows, :] = (1.0 - WEIGHT) * v + K[6, i, rows, :] * acc

    def residual(self, V, K, G, T, px, Xc, Y, a=0, b=None):
        V, K, G, T = (self.r[n] for n in (V, K, G, T))
        rows = slice(TOP, TOP + Y)

        @pl.loop(a, Xc if b is None else b)
        def _(j):
            for c in range(self.C):
                total = None
                for q in range(2):
                    i = px + 2 * j + q
                    v, acc = self.stencil(V, K, G, i, c, rows)
                    d = acc - K[7, i, rows, :] * v
                    total = d if total is None else total + d
                T[pl.ds(pl.multiple_of((c * Xc + j) * Y, 8), Y), :] = 0.5 * total

    def dot(self, a, b):
        return lax.dot_general(a, b, (((1,), (0,)), ((), ())), preferred_element_type=jnp.float32)

    def split(self, t):
        hi = t.astype(jnp.bfloat16)
        return hi, (t - hi.astype(jnp.float32)).astype(jnp.bfloat16)

    def right(self, t, m):
        hi, lo = self.split(t)
        return self.dot(hi, m) + self.dot(lo, m)

    def left(self, m, t):
        hi, lo = self.split(t)
        return self.dot(m, hi) + self.dot(m, lo)

    def pairs(self, n, m, value, fine_dim):
        r = lax.broadcasted_iota(jnp.int32, (n, m), 0)
        c = lax.broadcasted_iota(jnp.int32, (n, m), 1)
        hit = (r >> 1) == c if fine_dim == 0 else (c >> 1) == r
        return jnp.where(hit, value, 0.0).astype(jnp.bfloat16)

    def squeeze(self, t):
        rows, Z = t.shape
        half = self.right(t, self.pairs(Z, Z // 2, 0.5, 0))
        return self.left(self.pairs(rows // 2, rows, 0.5, 1), half)

    def prolong(self, W, a, count, U, V, planes, coarse_of, offset):
        W, U, V = (self.r[n] for n in (W, U, V))
        C, _, Rc, Zc = W.shape
        Rf, Zf = V.shape[-2:]
        src = W[:, a:a + count].reshape(C * count * Rc, Zc)
        U[...] = self.right(src, self.pairs(Zc, Zf, 1.0, 1))
        r = lax.broadcasted_iota(jnp.int32, (Rf, Rc), 0)
        c = lax.broadcasted_iota(jnp.int32, (Rf, Rc), 1)
        r = jnp.where(r < Rf - 4, r, r - Rf)
        c = c - offset if offset else jnp.where(c < Rc - 4, c, c - Rc)
        lift = jnp.where((r >> 1) == c, 1.0, 0.0).astype(jnp.bfloat16)
        for comp in range(C):
            for k in range(count):
                start = (comp * count + k) * Rc
                block = self.left(lift, U[start:start + Rc, :])
                for p in planes:
                    if coarse_of(p) == a + k:
                        V[comp, p] = V[comp, p] + block

    def body(self, forcing, phase, out, *scratch):
        names = list(self.scratch)
        self.r = r = dict(zip(names, scratch))
        self.ssem, self.rsem, lsem = scratch[len(names):]
        self.gx, self.gy = lax.axis_index("gx"), lax.axis_index("gy")
        X, Y, Z, C = self.X, self.Y, self.Z, self.C
        X1, Y1 = self.X1, self.Y1
        block = (pl.ds(2, X), pl.ds(TOP, Y))
        load_p = pltpu.make_async_copy(phase, r["ph"], lsem.at[0])
        load_p.start()
        for n in ("E0", "F0", "V0", "E1", "F1", "V1", "E2", "F2", "A2"):
            ref = r[n]
            for c in range(ref.shape[0]):
                @pl.loop(0, ref.shape[1])
                def _(i):
                    ref[c, i] = jnp.zeros(ref.shape[2:], jnp.float32)
        for n in list(r):
            if n.startswith("h") and n[-3:] in ("_ry", "_rd") or n in ("Re2", "Rf2", "Rv2"):
                ref = r[n]
                for k in range(ref.shape[0]):
                    ref[k] = jnp.zeros(ref.shape[1:], jnp.float32)
        load_f = pltpu.make_async_copy(forcing, r["F0"].at[:, block[0], block[1], :], lsem.at[1])
        load_f.start()

        barrier = pltpu.get_barrier_semaphore()
        count = jnp.int32(0)
        for dx, dy in WINDOW:
            ok = self.exists(dx, dy)
            count = count + ok.astype(jnp.int32)

            @pl.when(ok)
            def _():
                pl.semaphore_signal(barrier, inc=1, device_id=(self.gx + dx, self.gy + dy), device_id_type=MESH)
        load_p.wait()

        @pl.loop(0, X)
        def _(i):
            ph = r["ph"][i]
            e = jnp.zeros(ph.shape, jnp.float32)
            for k, value in enumerate(VISCOSITIES):
                e = jnp.where(ph == k, jnp.float32(value), e)
            r["E0"][0, i + 2, TOP:TOP + Y, :] = e
        pl.semaphore_wait(barrier, count)
        self.halo_start(self.hE0)
        load_f.wait()
        self.halo_start(self.hF0)

        for j in range(X1):
            r["T0"][j * Y:(j + 1) * Y, :] = 0.5 * (
                r["E0"][0, 2 + 2 * j, TOP:TOP + Y, :] + r["E0"][0, 3 + 2 * j, TOP:TOP + Y, :])
        e1 = self.squeeze(r["T0"][0:X1 * Y, :])
        for j in range(X1):
            r["E1"][0, 3 + j, TOP:TOP + Y1, :] = e1[j * Y1:(j + 1) * Y1]
        self.halo_start(self.hE1)
        for j in range(self.X2):
            r["T1"][j * Y1:(j + 1) * Y1, :] = 0.5 * (
                e1[2 * j * Y1:(2 * j + 1) * Y1] + e1[(2 * j + 1) * Y1:(2 * j + 2) * Y1])
        r["Se2"][...] = self.squeeze(r["T1"][0:self.X2 * Y1, :])
        self.win_start("e2")

        self.halo_wait(self.hE0, "y")
        self.coefs("E0", "C0", 3, X + 1, 1.0)
        self.halo_wait(self.hE0, "xd")
        self.coefs("E0", "C0", 1, 3, 1.0)
        self.coefs("E0", "C0", X + 1, X + 3, 1.0)
        self.halo_wait(self.hF0)
        self.first("C0", "F0", "A0", 1, X + 3)
        rows0 = slice(TOP, TOP + Y)
        self.sweep("A0", "C0", "F0", "V0", 2, 3, rows0)
        self.sweep("A0", "C0", "F0", "V0", X + 1, X + 2, rows0)
        self.halo_start(self.hV0, "x")
        self.sweep("A0", "C0", "F0", "V0", 3, X + 1, rows0)
        self.halo_start(self.hV0, "yd")
        self.halo_wait(self.hE1)
        self.coefs("E1", "C1", 1, X1 + 5, 4.0)
        self.win_wait("e2", "E2")
        self.coefs("E2", "C2", 1, self.X2 + 7, 16.0)
        self.halo_wait(self.hV0, "y")
        self.residual("V0", "C0", "F0", "T0", 2, X1, Y, 1, X1 - 1)
        self.halo_wait(self.hV0, "x")
        self.residual("V0", "C0", "F0", "T0", 2, X1, Y, 0, 1)
        self.residual("V0", "C0", "F0", "T0", 2, X1, Y, X1 - 1, X1)
        f1 = self.squeeze(r["T0"][...])
        for c in range(C):
            for j in range(X1):
                s = (c * X1 + j) * Y1
                r["F1"][c, 3 + j, TOP:TOP + Y1, :] = f1[s:s + Y1]

        self.halo_start(self.hF1)
        self.halo_wait(self.hF1)
        self.first("C1", "F1", "A1", 1, X1 + 5)
        self.sweep("A1", "C1", "F1", "B1", 2, X1 + 4)
        self.residual("B1", "C1", "F1", "T1", 3, self.X2, Y1)
        r["Sf2"][...] = self.squeeze(r["T1"][...])
        self.win_start("f2")
        for c in range(C):
            for j in range(X1):
                r["V1"][c, 3 + j, TOP:TOP + Y1, :] = r["B1"][c, 3 + j, TOP:TOP + Y1, :]
            for dx in (2, X1 + 3):
                r["V1"][c, dx, 0:Y1, :] = r["B1"][c, dx, 0:Y1, :]
            for j in range(-1, X1 + 1):
                for q in (self.R1 - 1, Y1):
                    r["V1"][c, 3 + j, q:q + 1, :] = r["B1"][c, 3 + j, q:q + 1, :]
        self.halo_start(self.hV1)

        self.win_wait("f2", "F2")
        p2 = self.P2
        self.first("C2", "F2", "A2", 1, p2 - 1)
        self.sweep("A2", "C2", "F2", "B2", 2, p2 - 2)
        self.sweep("B2", "C2", "F2", "A2", 3, p2 - 3)
        self.sweep("A2", "C2", "F2", "B2", 4, p2 - 4)
        for c in range(C):
            for p in range(self.X2):
                i = (c * self.X2 + p) * self.Y2
                r["Sv2"][i:i + self.Y2, :] = r["B2"][c, 4 + p, self.Y2:2 * self.Y2, :]
        self.win_start("v2")
        for h in self.hW0:
            self.halo_start(h)
        self.win_wait("v2", "A2")
        self.sweep("A2", "C2", "F2", "B2", 1, p2 - 1)
        self.sweep("B2", "C2", "F2", "A2", 2, p2 - 2)

        self.halo_wait(self.hV1)
        self.halo_sent(self.hV1)
        self.prolong("A2", 2, self.X2 + 4, "UZ1", "V1", range(self.P1),
                     lambda p: 4 + (p - 3) // 2, self.Y2)
        self.sweep("V1", "C1", "F1", "A1", 1, X1 + 5)
        self.sweep("A1", "C1", "F1", "B1", 2, X1 + 4)

        for h in self.hW0:
            self.halo_wait(h)
            self.halo_sent(h)
        self.halo_sent(self.hV0)
        self.prolong("B1", 2, X1 + 2, "UZ0", "V0", range(self.P0),
                     lambda p: 3 + (p - 2) // 2, 0)
        self.sweep("V0", "C0", "F0", "B0", 1, X + 3)
        self.sweep("B0", "C0", "F0", "O0", 2, X + 2, rows0, shift=2)
        store = pltpu.make_async_copy(r["O0"], out, lsem.at[0])
        store.start()
        for h in (self.hE0, self.hF0, self.hE1, self.hF1):
            self.halo_sent(h)
        for n in ("e2", "f2", "v2"):
            self.win_sent(n)
        store.wait()

    def __call__(self, forcing, phase):
        any_space = pl.BlockSpec(memory_space=pl.ANY)
        sems = [pltpu.SemaphoreType.DMA((self.n_sems,)), pltpu.SemaphoreType.DMA((self.n_sems,)),
                pltpu.SemaphoreType.DMA((2,))]
        return pl.pallas_call(
            self.body,
            out_shape=jax.ShapeDtypeStruct(forcing.shape, jnp.float32),
            in_specs=[any_space, any_space],
            out_specs=any_space,
            scratch_shapes=list(self.scratch.values()) + sems,
            compiler_params=pltpu.CompilerParams(
                collective_id=0, has_side_effects=True, vmem_limit_bytes=60 * 1024 * 1024),
            name="vcycle",
        )(forcing, phase)


def solution(mesh):
    grid = (mesh.shape["gx"], mesh.shape["gy"])

    def per_device(forcing, phase_ids):
        return Kernel(phase_ids.shape, forcing.shape[0], grid)(forcing, phase_ids)

    return jax.shard_map(
        per_device,
        mesh=mesh,
        in_specs=(P(None, "gx", "gy", None), P("gx", "gy", None)),
        out_specs=P(None, "gx", "gy", None),
        check_vma=False,
    )
```

```python
import functools

import jax
import jax.numpy as jnp
from jax import lax
from jax.experimental import pallas as pl
from jax.experimental.pallas import tpu as pltpu
from jax.sharding import PartitionSpec as P

COARSE_SWEEPS = 6
VISCOSITIES = (0.2, 0.6, 1.5, 4.0)
WEIGHT = 2.0 / 3.0
MESH = pl.DeviceIdType.MESH
WINDOW = [(dx, dy) for dx in range(-2, 3) for dy in range(-1, 2) if (dx, dy) != (0, 0)]
TOP = 0


def up8(n):
    return -(-n // 8) * 8


def side_slices(step, first, length, lo, hi):
    if step > 0:
        return (first + length - hi, first - hi)
    return (first + lo - 1, first + length + lo - 1)


class Kernel:
    def __init__(self, sizes, comps, grid):
        self.X, self.Y, self.Z = sizes
        self.C = comps
        self.grid = grid
        self.scratch = {}
        self.n_sems = 0
        self.plan()

    def buf(self, name, shape, dtype=jnp.float32):
        self.scratch[name] = pltpu.VMEM(tuple(shape), dtype)

    def halo(self, name, target, comps, px, X, Y, Z, lo, hi, diag, base=0):
        w = hi - lo + 1
        msgs = []
        for dx in (1, -1):
            s, d = side_slices(dx, px, X, lo, hi)
            msgs.append(("x", dx, 0, s, d, self.n_sems))
            self.n_sems += 1
        n = comps * X * w
        self.buf(name + "_sy", (2, up8(n), Z))
        self.buf(name + "_ry", (2, up8(n), Z))
        for k, dy in enumerate((1, -1)):
            s, d = side_slices(dy, TOP, Y, lo, hi)
            d %= Y + 8
            msgs.append(("y", k, dy, s, d, self.n_sems))
            self.n_sems += 1
        if diag:
            n = comps * len(diag)
            self.buf(name + "_sd", (4, n, 1, Z))
            self.buf(name + "_rd", (4, n, 1, Z))
            for k, (dx, dy) in enumerate([(1, 1), (1, -1), (-1, 1), (-1, -1)]):
                cells = [[], []]
                for a, b in diag:
                    sx, tx = side_slices(dx, px, X, a, a)
                    sy, ty = side_slices(dy, TOP, Y, b, b)
                    cells[0].append((sx, sy))
                    cells[1].append((tx, ty % (Y + 8)))
                msgs.append(("d", k, (dx, dy), cells[0], cells[1], self.n_sems))
                self.n_sems += 1
        return dict(name=name, base=base, target=target, comps=comps, px=px, X=X, Y=Y, w=w, diag=diag, msgs=msgs)

    def plan(self):
        X, Y, Z, C = self.X, self.Y, self.Z, self.C
        self.P0, self.R0 = X + 4, Y + 8
        self.X1, self.Y1, self.Z1 = X // 2, Y // 2, Z // 2
        self.P1, self.R1 = self.X1 + 6, self.Y1 + 8
        self.X2, self.Y2, self.Z2 = X // 4, Y // 4, Z // 4
        self.P2, self.R2 = self.X2 + 8, up8(self.Y2 * 3)
        b = self.buf
        b("ph", (X, Y, Z), jnp.int32)
        b("E0", (1, self.P0, self.R0, Z))
        b("C0", (8, self.P0, self.R0, Z))
        for n in ("F0", "A0", "V0", "B0"):
            b(n, (C, self.P0, self.R0, Z))
        b("O0", (C, X, Y, Z))
        b("T0", (C * self.X1 * Y, Z))
        b("E1", (1, self.P1, self.R1, self.Z1))
        b("C1", (8, self.P1, self.R1, self.Z1))
        for n in ("F1", "A1", "V1", "B1"):
            b(n, (C, self.P1, self.R1, self.Z1))
        b("T1", (C * self.X2 * self.Y1, self.Z1))
        b("E2", (1, self.P2, self.R2, self.Z2))
        b("C2", (8, self.P2, self.R2, self.Z2))
        for n in ("F2", "A2", "B2"):
            b(n, (C, self.P2, self.R2, self.Z2))
        blk = self.X2 * self.Y2
        for n, c in (("e2", 1), ("f2", C), ("v2", C)):
            b("S" + n, (c * blk, self.Z2))
            b("R" + n, (len(WINDOW), c * blk, self.Z2))
        b("UZ1", (self.R2 * C * (self.X2 + 4), self.Z1))
        b("UZ0", (self.R1 * C * (self.X1 + 2), self.Z))
        reach = [(1, 1), (1, 2), (2, 1), (1, 3), (2, 2), (3, 1)]
        self.hE0 = self.halo("hE0", "E0", 1, 2, X, Y, Z, 1, 2, [(1, 1)])
        self.hF0 = [self.halo("hFc%d" % c, "F0", 1, 2, X, Y, Z, 1, 1, [], c) for c in range(C)]
        self.hV0 = [self.halo("hVc%d" % c, "V0", 1, 2, X, Y, Z, 1, 1, [], c) for c in range(C)]
        self.hW0 = [self.halo("hW%d" % c, "V0", 1, 2, X, Y, Z, 2, 2, [(1, 1)], c) for c in range(C)]
        self.hE1 = self.halo("hE1", "E1", 1, 3, self.X1, self.Y1, self.Z1, 1, 3, reach)
        self.hF1 = self.halo("hF1", "F1", C, 3, self.X1, self.Y1, self.Z1, 1, 2, reach[:3])
        self.hV1 = self.halo("hV1", "V1", C, 3, self.X1, self.Y1, self.Z1, 2, 3, reach[1:])
        self.win = {}
        for n in ("e2", "f2", "v2"):
            self.win[n] = self.n_sems
            self.n_sems += len(WINDOW)

    def exists(self, dx, dy):
        ok = None
        for step, me, size in ((dx, self.gx, self.grid[0]), (dy, self.gy, self.grid[1])):
            if step:
                t = (me + step >= 0) & (me + step < size)
                ok = t if ok is None else ok & t
        return ok

    def copy(self, src, dst, sem, dx, dy):
        return pltpu.make_async_remote_copy(
            src_ref=src, dst_ref=dst, send_sem=self.ssem.at[sem], recv_sem=self.rsem.at[sem],
            device_id=(self.gx + dx, self.gy + dy), device_id_type=MESH)

    def halo_copies(self, h, kinds="xyd"):
        r = self.r
        ref = r[h["target"]]
        rows = pl.ds(TOP, h["Y"])
        out = []
        for m in h["msgs"]:
            if m[0] not in kinds:
                continue
            if m[0] == "x":
                _, dx, dy, s, d, sem = m
                comps = pl.ds(h["base"], h["comps"])
                c = self.copy(ref.at[comps, pl.ds(s, h["w"]), rows, :], ref.at[comps, pl.ds(d, h["w"]), rows, :],
                              sem, dx, 0)
                out.append((c, dx, 0))
            elif m[0] == "y":
                _, k, dy, s, d, sem = m
                out.append((self.copy(r[h["name"] + "_sy"].at[k], r[h["name"] + "_ry"].at[k], sem, 0, dy), 0, dy))
            else:
                _, k, (dx, dy), _, _, sem = m
                out.append((self.copy(r[h["name"] + "_sd"].at[k], r[h["name"] + "_rd"].at[k], sem, dx, dy), dx, dy))
        return out

    def rows_of(self, h, m, which):
        if m[0] == "y":
            start = m[3 + which]
            return m[1], "y", [(c + h["base"], h["px"] + p, start + q) for c in range(h["comps"])
                               for p in range(h["X"]) for q in range(h["w"])]
        return m[1], "d", [(c + h["base"], p, q) for c in range(h["comps"]) for p, q in m[3 + which]]

    def halo_start(self, h, kinds="xyd"):
        ref = self.r[h["target"]]
        for m in h["msgs"]:
            if m[0] == "x" or m[0] not in kinds:
                continue
            k, kind, rows = self.rows_of(h, m, 0)
            stage = self.r[h["name"] + "_s" + kind]
            for i, (c, p, q) in enumerate(rows):
                row = ref[c, p, q:q + 1, :]
                if kind == "d":
                    stage[k, i] = row
                else:
                    stage[k, i:i + 1, :] = row
        for c, dx, dy in self.halo_copies(h, kinds):
            pl.when(self.exists(dx, dy))(c.start)

    def halo_wait(self, h, kinds="xyd"):
        ref = self.r[h["target"]]
        for c, dx, dy in self.halo_copies(h, kinds):
            pl.when(self.exists(-dx, -dy))(c.wait_recv)
        for m in h["msgs"]:
            if m[0] == "x" or m[0] not in kinds:
                continue
            k, kind, rows = self.rows_of(h, m, 1)
            stage = self.r[h["name"] + "_r" + kind]
            for i, (c, p, q) in enumerate(rows):
                ref[c, p, q:q + 1, :] = stage[k, i] if kind == "d" else stage[k, i:i + 1, :]

    def halo_sent(self, h):
        for c, dx, dy in self.halo_copies(h):
            pl.when(self.exists(dx, dy))(c.wait_send)

    def win_copies(self, n):
        src, dst = self.r["S" + n], self.r["R" + n]
        return [(self.copy(src, dst.at[k], self.win[n] + k, dx, dy), dx, dy) for k, (dx, dy) in enumerate(WINDOW)]

    def win_start(self, n):
        for c, dx, dy in self.win_copies(n):
            pl.when(self.exists(dx, dy))(c.start)

    def win_wait(self, n, target):
        copies = self.win_copies(n)
        for c, dx, dy in copies:
            pl.when(self.exists(-dx, -dy))(c.wait_recv)
        ref = self.r[target]
        X2, Y2 = self.X2, self.Y2
        for k, (dx, dy) in enumerate(WINDOW + [(0, 0)]):
            for c in range(ref.shape[0]):
                for p in range(X2):
                    i = (c * X2 + p) * Y2
                    if (dx, dy) == (0, 0):
                        v = self.r["S" + n][i:i + Y2, :]
                    else:
                        v = self.r["R" + n][k, i:i + Y2, :]
                    ref[c, 4 + p - dx * X2, Y2 * (1 - dy):Y2 * (2 - dy), :] = v

    def win_sent(self, n):
        for c, dx, dy in self.win_copies(n):
            pl.when(self.exists(dx, dy))(c.wait_send)

    def coefs(self, E, K, a, b, scale):
        E, K = self.r[E], self.r[K]
        Z = E.shape[-1]
        shape = E.shape[-2:]
        R = shape[0]
        s = 1.0 / scale

        @pl.loop(a, b)
        def _(i):
            z = lax.broadcasted_iota(jnp.int32, shape, 1)
            e = E[0, i]

            def face(o):
                t = e + o
                return jnp.where(jnp.minimum(e, o) > 0.0, t * (0.5 * s), t * s)

            zp = jnp.where(z == Z - 1, 0.0, pltpu.roll(e, Z - 1, 1))
            zm = jnp.where(z == 0, 0.0, pltpu.roll(e, 1, 1))
            others = (E[0, i + 1], E[0, i - 1], pltpu.roll(e, R - 1, 0), pltpu.roll(e, 1, 0), zp, zm)
            diag = None
            for k, o in enumerate(others):
                c = face(o)
                diag = c if diag is None else diag + c
                if k == 4:
                    c = jnp.where(z == Z - 1, 0.0, c)
                if k == 5:
                    c = jnp.where(z == 0, 0.0, c)
                K[k, i] = c
            inside = e > 0.0
            K[6, i] = jnp.where(inside, WEIGHT / jnp.where(inside, diag, 1.0), 0.0)
            K[7, i] = diag

    def stencil(self, V, K, G, i, c, rows):
        R, Z = V.shape[-2:]
        n = rows.stop - rows.start
        v = V[c, i, rows, :]
        if n == R:
            yp, ym = pltpu.roll(v, R - 1, 0), pltpu.roll(v, 1, 0)
        else:
            yp, ym = V[c, i, 1:n + 1, :], pltpu.roll(V[c, i], 1, 0)[:n]
        acc = G[c, i, rows, :]
        parts = (V[c, i + 1, rows, :], V[c, i - 1, rows, :], yp, ym, pltpu.roll(v, Z - 1, 1), pltpu.roll(v, 1, 1))
        for k, o in enumerate(parts):
            acc = acc + K[k, i, rows, :] * o
        return v, acc

    def first(self, K, G, O, a, b, comps=None):
        K, G, O = (self.r[n] for n in (K, G, O))

        @pl.loop(a, b)
        def _(i):
            w = K[6, i]
            for c in comps or range(self.C):
                O[c, i] = w * G[c, i]

    def sweep(self, V, K, G, O, a, b, rows=None, shift=0, comps=None):
        V, K, G, O = (self.r[n] for n in (V, K, G, O))
        rows = rows or slice(0, V.shape[-2])
        out_rows = rows if shift == 0 else slice(0, rows.stop - rows.start)

        @pl.loop(a, b)
        def _(i):
            for c in comps or range(self.C):
                v, acc = self.stencil(V, K, G, i, c, rows)
                O[c, i - shift, out_rows, :] = (1.0 - WEIGHT) * v + K[6, i, rows, :] * acc

    def residual(self, V, K, G, T, px, Xc, Y, a=0, b=None, comps=None):
        V, K, G, T = (self.r[n] for n in (V, K, G, T))
        rows = slice(TOP, TOP + Y)

        @pl.loop(a, Xc if b is None else b)
        def _(j):
            for c in comps or range(self.C):
                total = None
                for q in range(2):
                    i = px + 2 * j + q
                    v, acc = self.stencil(V, K, G, i, c, rows)
                    d = acc - K[7, i, rows, :] * v
                    total = d if total is None else total + d
                T[pl.ds(pl.multiple_of((c * Xc + j) * Y, 8), Y), :] = 0.5 * total

    def dot(self, a, b):
        return lax.dot_general(a, b, (((1,), (0,)), ((), ())), preferred_element_type=jnp.float32)

    def split(self, t):
        hi = t.astype(jnp.bfloat16)
        return hi, (t - hi.astype(jnp.float32)).astype(jnp.bfloat16)

    def right(self, t, m):
        hi, lo = self.split(t)
        return self.dot(hi, m) + self.dot(lo, m)

    def left(self, m, t):
        hi, lo = self.split(t)
        return self.dot(m, hi) + self.dot(m, lo)

    def pairs(self, n, m, value, fine_dim):
        r = lax.broadcasted_iota(jnp.int32, (n, m), 0)
        c = lax.broadcasted_iota(jnp.int32, (n, m), 1)
        hit = (r >> 1) == c if fine_dim == 0 else (c >> 1) == r
        return jnp.where(hit, value, 0.0).astype(jnp.bfloat16)

    def squeeze(self, t):
        rows, Z = t.shape
        half = self.right(t, self.pairs(Z, Z // 2, 0.5, 0))
        return self.left(self.pairs(rows // 2, rows, 0.5, 1), half)

    def prolong(self, W, a, count, U, V, planes, coarse_of, offset):
        W, U, V = (self.r[n] for n in (W, U, V))
        C, _, Rc, Zc = W.shape
        Rf, Zf = V.shape[-2:]
        src = W[:, a:a + count].reshape(C * count * Rc, Zc)
        U[...] = self.right(src, self.pairs(Zc, Zf, 1.0, 1))
        r = lax.broadcasted_iota(jnp.int32, (Rf, Rc), 0)
        c = lax.broadcasted_iota(jnp.int32, (Rf, Rc), 1)
        r = jnp.where(r < Rf - 4, r, r - Rf)
        c = c - offset if offset else jnp.where(c < Rc - 4, c, c - Rc)
        lift = jnp.where((r >> 1) == c, 1.0, 0.0).astype(jnp.bfloat16)
        for comp in range(C):
            for k in range(count):
                start = (comp * count + k) * Rc
                block = self.left(lift, U[start:start + Rc, :])
                for p in planes:
                    if coarse_of(p) == a + k:
                        V[comp, p] = V[comp, p] + block

    def body(self, forcing, phase, out, *scratch):
        names = list(self.scratch)
        self.r = r = dict(zip(names, scratch))
        self.ssem, self.rsem, lsem = scratch[len(names):]
        self.gx, self.gy = lax.axis_index("gx"), lax.axis_index("gy")
        X, Y, Z, C = self.X, self.Y, self.Z, self.C
        X1, Y1 = self.X1, self.Y1
        block = (pl.ds(2, X), pl.ds(TOP, Y))
        load_p = pltpu.make_async_copy(phase, r["ph"], lsem.at[0])
        load_p.start()
        for n in ("E0", "F0", "V0", "E1", "F1", "V1", "E2", "F2", "A2"):
            ref = r[n]
            for c in range(ref.shape[0]):
                @pl.loop(0, ref.shape[1])
                def _(i):
                    ref[c, i] = jnp.zeros(ref.shape[2:], jnp.float32)
        for n in list(r):
            if n.startswith("h") and n[-3:] in ("_ry", "_rd") or n in ("Re2", "Rf2", "Rv2"):
                ref = r[n]
                for k in range(ref.shape[0]):
                    ref[k] = jnp.zeros(ref.shape[1:], jnp.float32)
        load_f = pltpu.make_async_copy(forcing, r["F0"].at[:, block[0], block[1], :], lsem.at[1])
        load_f.start()

        barrier = pltpu.get_barrier_semaphore()
        count = jnp.int32(0)
        for dx, dy in WINDOW:
            ok = self.exists(dx, dy)
            count = count + ok.astype(jnp.int32)

            @pl.when(ok)
            def _():
                pl.semaphore_signal(barrier, inc=1, device_id=(self.gx + dx, self.gy + dy), device_id_type=MESH)
        load_p.wait()

        @pl.loop(0, X)
        def _(i):
            ph = r["ph"][i]
            e = jnp.zeros(ph.shape, jnp.float32)
            for k, value in enumerate(VISCOSITIES):
                e = jnp.where(ph == k, jnp.float32(value), e)
            r["E0"][0, i + 2, TOP:TOP + Y, :] = e
        pl.semaphore_wait(barrier, count)
        self.halo_start(self.hE0)
        load_f.wait()
        for h in self.hF0:
            self.halo_start(h)

        for j in range(X1):
            r["T0"][j * Y:(j + 1) * Y, :] = 0.5 * (
                r["E0"][0, 2 + 2 * j, TOP:TOP + Y, :] + r["E0"][0, 3 + 2 * j, TOP:TOP + Y, :])
        e1 = self.squeeze(r["T0"][0:X1 * Y, :])
        for j in range(X1):
            r["E1"][0, 3 + j, TOP:TOP + Y1, :] = e1[j * Y1:(j + 1) * Y1]
        for j in range(self.X2):
            r["T1"][j * Y1:(j + 1) * Y1, :] = 0.5 * (
                e1[2 * j * Y1:(2 * j + 1) * Y1] + e1[(2 * j + 1) * Y1:(2 * j + 2) * Y1])
        r["Se2"][...] = self.squeeze(r["T1"][0:self.X2 * Y1, :])

        self.halo_wait(self.hE0, "y")
        self.coefs("E0", "C0", 3, X + 1, 1.0)
        self.halo_wait(self.hE0, "xd")
        self.coefs("E0", "C0", 1, 3, 1.0)
        self.coefs("E0", "C0", X + 1, X + 3, 1.0)
        rows0 = slice(TOP, TOP + Y)
        for c in range(C):
            self.halo_wait(self.hF0[c])
            self.first("C0", "F0", "A0", 1, X + 3, [c])
            self.sweep("A0", "C0", "F0", "V0", 2, 3, rows0, comps=[c])
            self.sweep("A0", "C0", "F0", "V0", X + 1, X + 2, rows0, comps=[c])
            self.halo_start(self.hV0[c], "x")
        self.sweep("A0", "C0", "F0", "V0", 3, X + 1, rows0)
        for h in self.hV0:
            self.halo_start(h, "y")
        self.halo_start(self.hE1)
        self.win_start("e2")
        for h in self.hV0:
            self.halo_wait(h, "y")
        self.residual("V0", "C0", "F0", "T0", 2, X1, Y, 1, X1 - 1)
        for c in range(C):
            self.halo_wait(self.hV0[c], "x")
            self.residual("V0", "C0", "F0", "T0", 2, X1, Y, 0, 1, [c])
            self.residual("V0", "C0", "F0", "T0", 2, X1, Y, X1 - 1, X1, [c])
        f1 = self.squeeze(r["T0"][...])
        for c in range(C):
            for j in range(X1):
                s = (c * X1 + j) * Y1
                r["F1"][c, 3 + j, TOP:TOP + Y1, :] = f1[s:s + Y1]

        self.halo_start(self.hF1)
        self.halo_wait(self.hE1)
        self.coefs("E1", "C1", 1, X1 + 5, 4.0)
        self.halo_wait(self.hF1)
        self.first("C1", "F1", "A1", 1, X1 + 5)
        self.sweep("A1", "C1", "F1", "B1", 2, X1 + 4)
        self.residual("B1", "C1", "F1", "T1", 3, self.X2, Y1)
        r["Sf2"][...] = self.squeeze(r["T1"][...])
        self.win_start("f2")
        for c in range(C):
            for j in range(X1):
                r["V1"][c, 3 + j, TOP:TOP + Y1, :] = r["B1"][c, 3 + j, TOP:TOP + Y1, :]
            for dx in (2, X1 + 3):
                r["V1"][c, dx, 0:Y1, :] = r["B1"][c, dx, 0:Y1, :]
            for j in range(-1, X1 + 1):
                for q in (self.R1 - 1, Y1):
                    r["V1"][c, 3 + j, q:q + 1, :] = r["B1"][c, 3 + j, q:q + 1, :]
        self.halo_start(self.hV1)

        self.win_wait("e2", "E2")
        self.coefs("E2", "C2", 1, self.X2 + 7, 16.0)
        self.win_wait("f2", "F2")
        p2 = self.P2
        self.first("C2", "F2", "A2", 1, p2 - 1)
        self.sweep("A2", "C2", "F2", "B2", 2, p2 - 2)
        self.sweep("B2", "C2", "F2", "A2", 3, p2 - 3)
        self.sweep("A2", "C2", "F2", "B2", 4, p2 - 4)
        for c in range(C):
            for p in range(self.X2):
                i = (c * self.X2 + p) * self.Y2
                r["Sv2"][i:i + self.Y2, :] = r["B2"][c, 4 + p, self.Y2:2 * self.Y2, :]
        self.win_start("v2")
        for h in self.hW0:
            self.halo_start(h)
        self.win_wait("v2", "A2")
        self.sweep("A2", "C2", "F2", "B2", 1, p2 - 1)
        self.sweep("B2", "C2", "F2", "A2", 2, p2 - 2)

        self.halo_wait(self.hV1)
        self.halo_sent(self.hV1)
        self.prolong("A2", 2, self.X2 + 4, "UZ1", "V1", range(self.P1),
                     lambda p: 4 + (p - 3) // 2, self.Y2)
        self.sweep("V1", "C1", "F1", "A1", 1, X1 + 5)
        self.sweep("A1", "C1", "F1", "B1", 2, X1 + 4)

        for h in self.hW0:
            self.halo_wait(h)
            self.halo_sent(h)
        for h in self.hV0:
            self.halo_sent(h)
        self.prolong("B1", 2, X1 + 2, "UZ0", "V0", range(self.P0),
                     lambda p: 3 + (p - 2) // 2, 0)
        self.sweep("V0", "C0", "F0", "B0", 1, X + 3)
        self.sweep("B0", "C0", "F0", "O0", 2, X + 2, rows0, shift=2)
        store = pltpu.make_async_copy(r["O0"], out, lsem.at[0])
        store.start()
        for h in (self.hE0, *self.hF0, self.hE1, self.hF1):
            self.halo_sent(h)
        for n in ("e2", "f2", "v2"):
            self.win_sent(n)
        store.wait()

    def __call__(self, forcing, phase):
        any_space = pl.BlockSpec(memory_space=pl.ANY)
        sems = [pltpu.SemaphoreType.DMA((self.n_sems,)), pltpu.SemaphoreType.DMA((self.n_sems,)),
                pltpu.SemaphoreType.DMA((2,))]
        return pl.pallas_call(
            self.body,
            out_shape=jax.ShapeDtypeStruct(forcing.shape, jnp.float32),
            in_specs=[any_space, any_space],
            out_specs=any_space,
            scratch_shapes=list(self.scratch.values()) + sems,
            compiler_params=pltpu.CompilerParams(
                collective_id=0, has_side_effects=True, vmem_limit_bytes=60 * 1024 * 1024),
            name="vcycle",
        )(forcing, phase)


def solution(mesh):
    grid = (mesh.shape["gx"], mesh.shape["gy"])

    def per_device(forcing, phase_ids):
        return Kernel(phase_ids.shape, forcing.shape[0], grid)(forcing, phase_ids)

    return jax.shard_map(
        per_device,
        mesh=mesh,
        in_specs=(P(None, "gx", "gy", None), P("gx", "gy", None)),
        out_specs=P(None, "gx", "gy", None),
        check_vma=False,
    )
```

```python
import functools

import jax
import jax.numpy as jnp
from jax import lax
from jax.experimental import pallas as pl
from jax.experimental.pallas import tpu as pltpu
from jax.sharding import PartitionSpec as P

COARSE_SWEEPS = 6
VISCOSITIES = (0.2, 0.6, 1.5, 4.0)
WEIGHT = 2.0 / 3.0
MESH = pl.DeviceIdType.MESH
WINDOW = [(dx, dy) for dx in range(-2, 3) for dy in range(-1, 2) if (dx, dy) != (0, 0)]
TOP = 0


def up8(n):
    return -(-n // 8) * 8


def side_slices(step, first, length, lo, hi):
    if step > 0:
        return (first + length - hi, first - hi)
    return (first + lo - 1, first + length + lo - 1)


class Kernel:
    def __init__(self, sizes, comps, grid):
        self.X, self.Y, self.Z = sizes
        self.C = comps
        self.grid = grid
        self.scratch = {}
        self.n_sems = 0
        self.plan()

    def buf(self, name, shape, dtype=jnp.float32):
        self.scratch[name] = pltpu.VMEM(tuple(shape), dtype)

    def halo(self, name, target, comps, px, X, Y, Z, lo, hi, diag, base=0):
        w = hi - lo + 1
        msgs = []
        for dx in (1, -1):
            s, d = side_slices(dx, px, X, lo, hi)
            msgs.append(("x", dx, 0, s, d, self.n_sems))
            self.n_sems += 1
        n = comps * X * w
        self.buf(name + "_sy", (2, up8(n), Z))
        self.buf(name + "_ry", (2, up8(n), Z))
        for k, dy in enumerate((1, -1)):
            s, d = side_slices(dy, TOP, Y, lo, hi)
            d %= Y + 8
            msgs.append(("y", k, dy, s, d, self.n_sems))
            self.n_sems += 1
        if diag:
            n = comps * len(diag)
            self.buf(name + "_sd", (4, n, 1, Z))
            self.buf(name + "_rd", (4, n, 1, Z))
            for k, (dx, dy) in enumerate([(1, 1), (1, -1), (-1, 1), (-1, -1)]):
                cells = [[], []]
                for a, b in diag:
                    sx, tx = side_slices(dx, px, X, a, a)
                    sy, ty = side_slices(dy, TOP, Y, b, b)
                    cells[0].append((sx, sy))
                    cells[1].append((tx, ty % (Y + 8)))
                msgs.append(("d", k, (dx, dy), cells[0], cells[1], self.n_sems))
                self.n_sems += 1
        return dict(name=name, base=base, target=target, comps=comps, px=px, X=X, Y=Y, w=w, diag=diag, msgs=msgs)

    def plan(self):
        X, Y, Z, C = self.X, self.Y, self.Z, self.C
        self.P0, self.R0 = X + 4, Y + 8
        self.X1, self.Y1, self.Z1 = X // 2, Y // 2, Z // 2
        self.P1, self.R1 = self.X1 + 6, self.Y1 + 8
        self.X2, self.Y2, self.Z2 = X // 4, Y // 4, Z // 4
        self.P2, self.R2 = self.X2 + 8, up8(self.Y2 * 3)
        b = self.buf
        b("ph", (X, Y, Z), jnp.int32)
        b("E0", (1, self.P0, self.R0, Z))
        b("C0", (8, self.P0, self.R0, Z))
        for n in ("F0", "A0", "V0", "B0"):
            b(n, (C, self.P0, self.R0, Z))
        b("O0", (C, X, Y, Z))
        b("T0", (C * self.X1 * Y, Z))
        b("E1", (1, self.P1, self.R1, self.Z1))
        b("C1", (8, self.P1, self.R1, self.Z1))
        for n in ("F1", "A1", "V1", "B1"):
            b(n, (C, self.P1, self.R1, self.Z1))
        b("T1", (C * self.X2 * self.Y1, self.Z1))
        b("E2", (1, self.P2, self.R2, self.Z2))
        b("C2", (8, self.P2, self.R2, self.Z2))
        for n in ("F2", "A2", "B2"):
            b(n, (C, self.P2, self.R2, self.Z2))
        blk = self.X2 * self.Y2
        for n, c in (("e2", 1), ("f2", C), ("v2", C)):
            b("S" + n, (c * blk, self.Z2))
            b("R" + n, (len(WINDOW), c * blk, self.Z2))
        b("UZ1", (self.R2 * C * (self.X2 + 4), self.Z1))
        b("UZ0", (self.R1 * C * (self.X1 + 2), self.Z))
        reach = [(1, 1), (1, 2), (2, 1), (1, 3), (2, 2), (3, 1)]
        self.hE0 = self.halo("hE0", "E0", 1, 2, X, Y, Z, 1, 2, [(1, 1)])
        self.hF0 = [self.halo("hFc%d" % c, "F0", 1, 2, X, Y, Z, 1, 1, [], c) for c in range(C)]
        self.hV0 = [self.halo("hVc%d" % c, "V0", 1, 2, X, Y, Z, 1, 1, [], c) for c in range(C)]
        self.hW0 = [self.halo("hW%d" % c, "V0", 1, 2, X, Y, Z, 2, 2, [(1, 1)], c) for c in range(C)]
        self.hE1 = self.halo("hE1", "E1", 1, 3, self.X1, self.Y1, self.Z1, 1, 3, reach)
        self.hF1 = self.halo("hF1", "F1", C, 3, self.X1, self.Y1, self.Z1, 1, 2, reach[:3])
        self.hV1 = self.halo("hV1", "V1", C, 3, self.X1, self.Y1, self.Z1, 2, 3, reach[1:])
        self.win = {}
        for n in ("e2", "f2", "v2"):
            self.win[n] = self.n_sems
            self.n_sems += len(WINDOW)

    def exists(self, dx, dy):
        ok = None
        for step, me, size in ((dx, self.gx, self.grid[0]), (dy, self.gy, self.grid[1])):
            if step:
                t = (me + step >= 0) & (me + step < size)
                ok = t if ok is None else ok & t
        return ok

    def copy(self, src, dst, sem, dx, dy):
        return pltpu.make_async_remote_copy(
            src_ref=src, dst_ref=dst, send_sem=self.ssem.at[sem], recv_sem=self.rsem.at[sem],
            device_id=(self.gx + dx, self.gy + dy), device_id_type=MESH)

    def halo_copies(self, h, kinds="xyd"):
        r = self.r
        ref = r[h["target"]]
        rows = pl.ds(TOP, h["Y"])
        out = []
        for m in h["msgs"]:
            if m[0] not in kinds:
                continue
            if m[0] == "x":
                _, dx, dy, s, d, sem = m
                comps = pl.ds(h["base"], h["comps"])
                c = self.copy(ref.at[comps, pl.ds(s, h["w"]), rows, :], ref.at[comps, pl.ds(d, h["w"]), rows, :],
                              sem, dx, 0)
                out.append((c, dx, 0))
            elif m[0] == "y":
                _, k, dy, s, d, sem = m
                out.append((self.copy(r[h["name"] + "_sy"].at[k], r[h["name"] + "_ry"].at[k], sem, 0, dy), 0, dy))
            else:
                _, k, (dx, dy), _, _, sem = m
                out.append((self.copy(r[h["name"] + "_sd"].at[k], r[h["name"] + "_rd"].at[k], sem, dx, dy), dx, dy))
        return out

    def rows_of(self, h, m, which):
        if m[0] == "y":
            start = m[3 + which]
            return m[1], "y", [(c + h["base"], h["px"] + p, start + q) for c in range(h["comps"])
                               for p in range(h["X"]) for q in range(h["w"])]
        return m[1], "d", [(c + h["base"], p, q) for c in range(h["comps"]) for p, q in m[3 + which]]

    def halo_start(self, h, kinds="xyd"):
        ref = self.r[h["target"]]
        for m in h["msgs"]:
            if m[0] == "x" or m[0] not in kinds:
                continue
            k, kind, rows = self.rows_of(h, m, 0)
            stage = self.r[h["name"] + "_s" + kind]
            for i, (c, p, q) in enumerate(rows):
                row = ref[c, p, q:q + 1, :]
                if kind == "d":
                    stage[k, i] = row
                else:
                    stage[k, i:i + 1, :] = row
        for c, dx, dy in self.halo_copies(h, kinds):
            pl.when(self.exists(dx, dy))(c.start)

    def halo_wait(self, h, kinds="xyd"):
        ref = self.r[h["target"]]
        for c, dx, dy in self.halo_copies(h, kinds):
            pl.when(self.exists(-dx, -dy))(c.wait_recv)
        for m in h["msgs"]:
            if m[0] == "x" or m[0] not in kinds:
                continue
            k, kind, rows = self.rows_of(h, m, 1)
            stage = self.r[h["name"] + "_r" + kind]
            for i, (c, p, q) in enumerate(rows):
                ref[c, p, q:q + 1, :] = stage[k, i] if kind == "d" else stage[k, i:i + 1, :]

    def halo_sent(self, h):
        for c, dx, dy in self.halo_copies(h):
            pl.when(self.exists(dx, dy))(c.wait_send)

    def win_copies(self, n):
        src, dst = self.r["S" + n], self.r["R" + n]
        return [(self.copy(src, dst.at[k], self.win[n] + k, dx, dy), dx, dy) for k, (dx, dy) in enumerate(WINDOW)]

    def win_start(self, n):
        for c, dx, dy in self.win_copies(n):
            pl.when(self.exists(dx, dy))(c.start)

    def win_wait(self, n, target):
        copies = self.win_copies(n)
        for c, dx, dy in copies:
            pl.when(self.exists(-dx, -dy))(c.wait_recv)
        ref = self.r[target]
        X2, Y2 = self.X2, self.Y2
        for k, (dx, dy) in enumerate(WINDOW + [(0, 0)]):
            for c in range(ref.shape[0]):
                for p in range(X2):
                    i = (c * X2 + p) * Y2
                    if (dx, dy) == (0, 0):
                        v = self.r["S" + n][i:i + Y2, :]
                    else:
                        v = self.r["R" + n][k, i:i + Y2, :]
                    ref[c, 4 + p - dx * X2, Y2 * (1 - dy):Y2 * (2 - dy), :] = v

    def win_sent(self, n):
        for c, dx, dy in self.win_copies(n):
            pl.when(self.exists(dx, dy))(c.wait_send)

    def coefs(self, E, K, a, b, scale):
        E, K = self.r[E], self.r[K]
        Z = E.shape[-1]
        shape = E.shape[-2:]
        R = shape[0]
        s = 1.0 / scale

        @pl.loop(a, b)
        def _(i):
            z = lax.broadcasted_iota(jnp.int32, shape, 1)
            e = E[0, i]

            def face(o):
                t = e + o
                return jnp.where(jnp.minimum(e, o) > 0.0, t * (0.5 * s), t * s)

            zp = jnp.where(z == Z - 1, 0.0, pltpu.roll(e, Z - 1, 1))
            zm = jnp.where(z == 0, 0.0, pltpu.roll(e, 1, 1))
            others = (E[0, i + 1], E[0, i - 1], pltpu.roll(e, R - 1, 0), pltpu.roll(e, 1, 0), zp, zm)
            diag = None
            for k, o in enumerate(others):
                c = face(o)
                diag = c if diag is None else diag + c
                if k == 4:
                    c = jnp.where(z == Z - 1, 0.0, c)
                if k == 5:
                    c = jnp.where(z == 0, 0.0, c)
                K[k, i] = c
            inside = e > 0.0
            K[6, i] = jnp.where(inside, WEIGHT / jnp.where(inside, diag, 1.0), 0.0)
            K[7, i] = diag

    def stencil(self, V, K, G, i, c, rows):
        R, Z = V.shape[-2:]
        n = rows.stop - rows.start
        v = V[c, i, rows, :]
        if n == R:
            yp, ym = pltpu.roll(v, R - 1, 0), pltpu.roll(v, 1, 0)
        else:
            yp, ym = V[c, i, 1:n + 1, :], pltpu.roll(V[c, i], 1, 0)[:n]
        acc = G[c, i, rows, :]
        parts = (V[c, i + 1, rows, :], V[c, i - 1, rows, :], yp, ym, pltpu.roll(v, Z - 1, 1), pltpu.roll(v, 1, 1))
        for k, o in enumerate(parts):
            acc = acc + K[k, i, rows, :] * o
        return v, acc

    def first(self, K, G, O, a, b, comps=None):
        K, G, O = (self.r[n] for n in (K, G, O))

        @pl.loop(a, b)
        def _(i):
            w = K[6, i]
            for c in comps or range(self.C):
                O[c, i] = w * G[c, i]

    def sweep(self, V, K, G, O, a, b, rows=None, shift=0, comps=None):
        V, K, G, O = (self.r[n] for n in (V, K, G, O))
        rows = rows or slice(0, V.shape[-2])
        out_rows = rows if shift == 0 else slice(0, rows.stop - rows.start)

        @pl.loop(a, b)
        def _(i):
            for c in comps or range(self.C):
                v, acc = self.stencil(V, K, G, i, c, rows)
                O[c, i - shift, out_rows, :] = (1.0 - WEIGHT) * v + K[6, i, rows, :] * acc

    def residual(self, V, K, G, T, px, Xc, Y, a=0, b=None, comps=None):
        V, K, G, T = (self.r[n] for n in (V, K, G, T))
        rows = slice(TOP, TOP + Y)

        @pl.loop(a, Xc if b is None else b)
        def _(j):
            for c in comps or range(self.C):
                total = None
                for q in range(2):
                    i = px + 2 * j + q
                    v, acc = self.stencil(V, K, G, i, c, rows)
                    d = acc - K[7, i, rows, :] * v
                    total = d if total is None else total + d
                T[pl.ds(pl.multiple_of((c * Xc + j) * Y, 8), Y), :] = 0.5 * total

    def dot(self, a, b):
        return lax.dot_general(a, b, (((1,), (0,)), ((), ())), preferred_element_type=jnp.float32)

    def split(self, t):
        hi = t.astype(jnp.bfloat16)
        return hi, (t - hi.astype(jnp.float32)).astype(jnp.bfloat16)

    def right(self, t, m):
        hi, lo = self.split(t)
        return self.dot(hi, m) + self.dot(lo, m)

    def left(self, m, t):
        hi, lo = self.split(t)
        return self.dot(m, hi) + self.dot(m, lo)

    def pairs(self, n, m, value, fine_dim):
        r = lax.broadcasted_iota(jnp.int32, (n, m), 0)
        c = lax.broadcasted_iota(jnp.int32, (n, m), 1)
        hit = (r >> 1) == c if fine_dim == 0 else (c >> 1) == r
        return jnp.where(hit, value, 0.0).astype(jnp.bfloat16)

    def squeeze(self, t):
        rows, Z = t.shape
        half = self.right(t, self.pairs(Z, Z // 2, 0.5, 0))
        return self.left(self.pairs(rows // 2, rows, 0.5, 1), half)

    def prolong(self, W, a, count, U, V, planes, coarse_of, offset):
        W, U, V = (self.r[n] for n in (W, U, V))
        C, _, Rc, Zc = W.shape
        Rf, Zf = V.shape[-2:]
        src = W[:, a:a + count].reshape(C * count * Rc, Zc)
        U[...] = self.right(src, self.pairs(Zc, Zf, 1.0, 1))
        r = lax.broadcasted_iota(jnp.int32, (Rf, Rc), 0)
        c = lax.broadcasted_iota(jnp.int32, (Rf, Rc), 1)
        r = jnp.where(r < Rf - 4, r, r - Rf)
        c = c - offset if offset else jnp.where(c < Rc - 4, c, c - Rc)
        lift = jnp.where((r >> 1) == c, 1.0, 0.0).astype(jnp.bfloat16)
        for comp in range(C):
            for k in range(count):
                start = (comp * count + k) * Rc
                block = self.left(lift, U[start:start + Rc, :])
                for p in planes:
                    if coarse_of(p) == a + k:
                        V[comp, p] = V[comp, p] + block

    def body(self, forcing, phase, out, *scratch):
        names = list(self.scratch)
        self.r = r = dict(zip(names, scratch))
        self.ssem, self.rsem, lsem = scratch[len(names):]
        self.gx, self.gy = lax.axis_index("gx"), lax.axis_index("gy")
        X, Y, Z, C = self.X, self.Y, self.Z, self.C
        X1, Y1 = self.X1, self.Y1
        block = (pl.ds(2, X), pl.ds(TOP, Y))
        load_p = pltpu.make_async_copy(phase, r["ph"], lsem.at[0])
        load_p.start()
        for n in ("F0", "V0"):
            ref = r[n]
            for c in range(C):
                for p in (0, 1, X + 2, X + 3):
                    ref[c, p, 0:Y, :] = jnp.zeros((Y, Z), jnp.float32)

                @pl.loop(0, self.P0)
                def _(i):
                    ref[c, i, Y:self.R0, :] = jnp.zeros((self.R0 - Y, Z), jnp.float32)
        for n in ("E0", "E1", "F1", "V1", "E2", "F2", "A2"):
            ref = r[n]
            for c in range(ref.shape[0]):
                @pl.loop(0, ref.shape[1])
                def _(i):
                    ref[c, i] = jnp.zeros(ref.shape[2:], jnp.float32)
        for n in list(r):
            if n.startswith("h") and n[-3:] in ("_ry", "_rd") or n in ("Re2", "Rf2", "Rv2"):
                ref = r[n]
                for k in range(ref.shape[0]):
                    ref[k] = jnp.zeros(ref.shape[1:], jnp.float32)
        load_f = pltpu.make_async_copy(forcing, r["F0"].at[:, block[0], block[1], :], lsem.at[1])
        load_f.start()

        barrier = pltpu.get_barrier_semaphore()
        count = jnp.int32(0)
        for dx, dy in WINDOW:
            ok = self.exists(dx, dy)
            count = count + ok.astype(jnp.int32)

            @pl.when(ok)
            def _():
                pl.semaphore_signal(barrier, inc=1, device_id=(self.gx + dx, self.gy + dy), device_id_type=MESH)
        load_p.wait()

        @pl.loop(0, X)
        def _(i):
            ph = r["ph"][i]
            e = jnp.zeros(ph.shape, jnp.float32)
            for k, value in enumerate(VISCOSITIES):
                e = jnp.where(ph == k, jnp.float32(value), e)
            r["E0"][0, i + 2, TOP:TOP + Y, :] = e
        pl.semaphore_wait(barrier, count)
        self.halo_start(self.hE0)
        load_f.wait()
        for h in self.hF0:
            self.halo_start(h)

        for j in range(X1):
            r["T0"][j * Y:(j + 1) * Y, :] = 0.5 * (
                r["E0"][0, 2 + 2 * j, TOP:TOP + Y, :] + r["E0"][0, 3 + 2 * j, TOP:TOP + Y, :])
        e1 = self.squeeze(r["T0"][0:X1 * Y, :])
        for j in range(X1):
            r["E1"][0, 3 + j, TOP:TOP + Y1, :] = e1[j * Y1:(j + 1) * Y1]
        for j in range(self.X2):
            r["T1"][j * Y1:(j + 1) * Y1, :] = 0.5 * (
                e1[2 * j * Y1:(2 * j + 1) * Y1] + e1[(2 * j + 1) * Y1:(2 * j + 2) * Y1])
        r["Se2"][...] = self.squeeze(r["T1"][0:self.X2 * Y1, :])

        self.halo_wait(self.hE0, "y")
        self.coefs("E0", "C0", 3, X + 1, 1.0)
        self.halo_wait(self.hE0, "xd")
        self.coefs("E0", "C0", 1, 3, 1.0)
        self.coefs("E0", "C0", X + 1, X + 3, 1.0)
        rows0 = slice(TOP, TOP + Y)
        for c in range(C):
            self.halo_wait(self.hF0[c])
            self.first("C0", "F0", "A0", 1, X + 3, [c])
            self.sweep("A0", "C0", "F0", "V0", 2, 3, rows0, comps=[c])
            self.sweep("A0", "C0", "F0", "V0", X + 1, X + 2, rows0, comps=[c])
            self.halo_start(self.hV0[c], "x")
        self.sweep("A0", "C0", "F0", "V0", 3, X + 1, rows0)
        for h in self.hV0:
            self.halo_start(h, "y")
        self.halo_start(self.hE1)
        self.win_start("e2")
        for h in self.hV0:
            self.halo_wait(h, "y")
        self.residual("V0", "C0", "F0", "T0", 2, X1, Y, 1, X1 - 1)
        for c in range(C):
            self.halo_wait(self.hV0[c], "x")
            self.residual("V0", "C0", "F0", "T0", 2, X1, Y, 0, 1, [c])
            self.residual("V0", "C0", "F0", "T0", 2, X1, Y, X1 - 1, X1, [c])
        f1 = self.squeeze(r["T0"][...])
        for c in range(C):
            for j in range(X1):
                s = (c * X1 + j) * Y1
                r["F1"][c, 3 + j, TOP:TOP + Y1, :] = f1[s:s + Y1]

        self.halo_start(self.hF1)
        self.halo_wait(self.hE1)
        self.coefs("E1", "C1", 1, X1 + 5, 4.0)
        self.halo_wait(self.hF1)
        self.first("C1", "F1", "A1", 1, X1 + 5)
        self.sweep("A1", "C1", "F1", "B1", 2, X1 + 4)
        self.residual("B1", "C1", "F1", "T1", 3, self.X2, Y1)
        r["Sf2"][...] = self.squeeze(r["T1"][...])
        self.win_start("f2")
        for c in range(C):
            for j in range(X1):
                r["V1"][c, 3 + j, TOP:TOP + Y1, :] = r["B1"][c, 3 + j, TOP:TOP + Y1, :]
            for dx in (2, X1 + 3):
                r["V1"][c, dx, 0:Y1, :] = r["B1"][c, dx, 0:Y1, :]
            for j in range(-1, X1 + 1):
                for q in (self.R1 - 1, Y1):
                    r["V1"][c, 3 + j, q:q + 1, :] = r["B1"][c, 3 + j, q:q + 1, :]
        self.halo_start(self.hV1)
        self.halo_start(self.hW0[0])

        self.win_wait("e2", "E2")
        self.coefs("E2", "C2", 1, self.X2 + 7, 16.0)
        self.win_wait("f2", "F2")
        p2 = self.P2
        self.first("C2", "F2", "A2", 1, p2 - 1)
        self.sweep("A2", "C2", "F2", "B2", 2, p2 - 2)
        self.sweep("B2", "C2", "F2", "A2", 3, p2 - 3)
        self.sweep("A2", "C2", "F2", "B2", 4, p2 - 4)
        for c in range(C):
            for p in range(self.X2):
                i = (c * self.X2 + p) * self.Y2
                r["Sv2"][i:i + self.Y2, :] = r["B2"][c, 4 + p, self.Y2:2 * self.Y2, :]
        self.win_start("v2")
        for h in self.hW0[1:]:
            self.halo_start(h)
        self.win_wait("v2", "A2")
        self.sweep("A2", "C2", "F2", "B2", 1, p2 - 1)
        self.sweep("B2", "C2", "F2", "A2", 2, p2 - 2)

        self.halo_wait(self.hV1)
        self.halo_sent(self.hV1)
        self.prolong("A2", 2, self.X2 + 4, "UZ1", "V1", range(self.P1),
                     lambda p: 4 + (p - 3) // 2, self.Y2)
        self.sweep("V1", "C1", "F1", "A1", 1, X1 + 5)
        self.sweep("A1", "C1", "F1", "B1", 2, X1 + 4)

        for h in self.hW0:
            self.halo_wait(h)
            self.halo_sent(h)
        for h in self.hV0:
            self.halo_sent(h)
        self.prolong("B1", 2, X1 + 2, "UZ0", "V0", range(self.P0),
                     lambda p: 3 + (p - 2) // 2, 0)
        self.sweep("V0", "C0", "F0", "B0", 1, X + 3)
        self.sweep("B0", "C0", "F0", "O0", 2, X + 2, rows0, shift=2)
        store = pltpu.make_async_copy(r["O0"], out, lsem.at[0])
        store.start()
        for h in (self.hE0, *self.hF0, self.hE1, self.hF1):
            self.halo_sent(h)
        for n in ("e2", "f2", "v2"):
            self.win_sent(n)
        store.wait()

    def __call__(self, forcing, phase):
        any_space = pl.BlockSpec(memory_space=pl.ANY)
        sems = [pltpu.SemaphoreType.DMA((self.n_sems,)), pltpu.SemaphoreType.DMA((self.n_sems,)),
                pltpu.SemaphoreType.DMA((2,))]
        return pl.pallas_call(
            self.body,
            out_shape=jax.ShapeDtypeStruct(forcing.shape, jnp.float32),
            in_specs=[any_space, any_space],
            out_specs=any_space,
            scratch_shapes=list(self.scratch.values()) + sems,
            compiler_params=pltpu.CompilerParams(
                collective_id=0, has_side_effects=True, vmem_limit_bytes=60 * 1024 * 1024),
            name="vcycle",
        )(forcing, phase)


def solution(mesh):
    grid = (mesh.shape["gx"], mesh.shape["gy"])

    def per_device(forcing, phase_ids):
        return Kernel(phase_ids.shape, forcing.shape[0], grid)(forcing, phase_ids)

    return jax.shard_map(
        per_device,
        mesh=mesh,
        in_specs=(P(None, "gx", "gy", None), P("gx", "gy", None)),
        out_specs=P(None, "gx", "gy", None),
        check_vma=False,
    )
```
